256 devices in a mesh: depth: 8 (over z_lo, core), tile: 32 (over y, x, z_hi).
Axes of the slice: x: 4, y: 4, z: 8 (z_hi: 2, z_lo: 4; z = z_hi * 4 + z_lo), core: 2. Of those that a mesh axis runs over, the one named last changes fastest.
Arguments:
- volume: float32 [32, 1024, 1024], P('depth', 'tile'), may hold values from -6 to 6
- measured: float32 [3, 1024, 1024], P(None, 'tile'), may hold values from -12 to 12
- row_bank: float32 [256, 2, 33], replicated, may hold values from -0.5 to 0.5
- col_bank: float32 [256, 2, 33], replicated, may hold values from -0.5 to 0.5
- kernel_index: int32 [169, 32], P(None, 'depth'), may hold values from 0 to 255
- view_order: int32 [3], replicated, may hold values from 0 to 168
Outputs:
- volume_out: float32 [32, 1024, 1024], P('depth', 'tile')
- last_residual: float32 [1024, 1024], P('tile')
The draws below stay inside these ranges and needn't reach their ends.
All inputs are finite; a program needn't handle non-finite values.
Results may differ from the reference program's by a relative error of at most 0.00013.
Values sent between devices are 32-bit elements; how exact they have to be, the bound alone decides.
A program may use at most 64 MiB of HBM per device.

```python
import jax
import jax.numpy as jnp
from jax import lax

WIDTH = 1024
TAPS = 33
BANK = 256
VIEWS = 169
NV = 3
DEPTH = 32
HEIGHT = 1024


def with_ends(result, key, smallest, largest):
    longest = result.shape.index(max(result.shape))
    spots = []
    for shift in (0, 1):
        where = [jax.random.randint(jax.random.fold_in(key, axis), (), 0, length) for axis, length in enumerate(result.shape)]
        where[longest] = (where[longest] + shift) % result.shape[longest]
        spots.append(tuple(where))
    return result.at[spots[0]].set(smallest).at[spots[1]].set(largest)


def block_scale(rng, extent, shards, smallest, largest):
    gain, own = 1.0, jax.random.fold_in(rng, 6)
    for dim, blocks in shards:
        heights = jnp.exp(jax.random.uniform(jax.random.fold_in(own, dim), (blocks,), jnp.float32, smallest / len(shards), largest / len(shards)))
        gain = gain * jnp.repeat(heights, extent[dim] // blocks).reshape([-1 if axis == dim else 1 for axis in range(len(extent))])
    return gain


def normal_values(stream_key, dims, scale, most, split=(), kind=jnp.bfloat16):
    array = jax.random.normal(stream_key, dims, jnp.float32) * scale
    if len(split) > 0:
        array = block_scale(stream_key, dims, split, -0.22, 0.18) * array
    return jnp.clip(array, min=-most, max=most).astype(kind)


def setup_inputs(seed: int = 0) -> dict:
    streams_of = jax.random.split(jax.random.key(seed), 7)
    volume = normal_values(streams_of[0], (DEPTH, HEIGHT, WIDTH), 1.0, 6.0, ((0, 8), (1, 32)), jnp.float32)
    measured = normal_values(streams_of[1], (NV, HEIGHT, WIDTH), 2.0, 12.0, ((1, 32),), jnp.float32)
    row_bank = normal_values(streams_of[2], (BANK, 2, TAPS), (33 * 2 * DEPTH // 14) ** -0.5, 0.5, (), jnp.float32)
    col_bank = normal_values(streams_of[3], (BANK, 2, TAPS), (33 * 2 * DEPTH // 14) ** -0.5, 0.5, (), jnp.float32)
    kernel_index = with_ends(jax.random.randint(streams_of[4], (VIEWS, DEPTH), 0, BANK), jax.random.fold_in(streams_of[4], 1), 0, BANK - 1).astype(jnp.int32)
    view_order = jax.random.randint(streams_of[5], (NV,), 0, VIEWS).astype(jnp.int32)
    return dict(volume=volume, measured=measured, row_bank=row_bank, col_bank=col_bank, kernel_index=kernel_index, view_order=view_order)


descent_step = 0.5
shrinkage = 0.1


def row_pass(extended, taps, rows):
    total = taps[:, :, 0, None, None] * extended[:, :, 0:rows, :]
    for shift_k in range(1, taps.shape[2]):
        total = total + taps[:, :, shift_k, None, None] * extended[:, :, shift_k:shift_k + rows, :]
    return total


def col_pass(upper, taps):
    width = upper.shape[3]
    reach = (taps.shape[2] - 1) // 2
    padded = jnp.pad(upper, ((0, 0), (0, 0), (0, 0), (reach, reach)))
    total = taps[:, :, 0, None, None] * padded[:, :, :, 0:width]
    for shift_k in range(1, taps.shape[2]):
        total = total + taps[:, :, shift_k, None, None] * padded[:, :, :, shift_k:shift_k + width]
    return total


def reference(volume, measured, row_bank, col_bank, kernel_index, view_order):
    reach = (row_bank.shape[2] - 1) // 2
    height = volume.shape[1]
    width = volume.shape[2]
    residual = jnp.zeros((height, width), jnp.float32)
    for step in range(measured.shape[0]):
        entries = kernel_index[view_order[step]]
        row_taps = jnp.take(row_bank, entries, axis=0)
        col_taps = jnp.take(col_bank, entries, axis=0)

        def add_plane(total, items):
            plane, row_one, col_one = items
            extended = jnp.pad(plane, ((reach, reach), (0, 0)))
            upper = row_pass(extended[None, None], row_one[None], height)
            return total + jnp.sum(col_pass(upper, col_one[None]), axis=(0, 1)), None

        image, _ = lax.scan(add_plane, jnp.zeros((height, width), jnp.float32), (volume, row_taps, col_taps))
        residual = image - measured[step]
        res_ext = jnp.pad(residual, ((reach, reach), (0, 0)))

        def update(items):
            plane, row_one, col_one = items
            upper = row_pass(res_ext[None, None], row_one[None, :, ::-1], height)
            grad = jnp.sum(col_pass(upper, col_one[None, :, ::-1]), axis=(0, 1))
            moved = plane - descent_step * grad
            return moved - jnp.clip(moved, -shrinkage, shrinkage)

        volume = lax.map(update, (volume, row_taps, col_taps))
    return volume, residual
```

```python
import functools

import jax
import jax.numpy as jnp
from jax import lax
from jax.experimental import pallas as pl
from jax.experimental.pallas import tpu as pltpu
from jax.sharding import PartitionSpec as P

MESH = pl.DeviceIdType.MESH
DESCENT = 0.5
SHRINK = 0.1
LANES = 128
F32, BF16 = jnp.float32, jnp.bfloat16


def split(x):
    hi = x.astype(BF16)
    return hi, (x - hi.astype(F32)).astype(BF16)


def dot(a, b):
    return jnp.dot(a, b, preferred_element_type=F32)


def lane_of(shape):
    return lax.broadcasted_iota(jnp.int32, shape, len(shape) - 1)


def sheared(row, rows):
    wide = jnp.broadcast_to(row, (rows, row.shape[1]))
    return pltpu.roll(wide, 0, 1, stride=1, stride_axis=0)


def kernel(
    nt, steps,
    vol, meas, rowb, colb, kidx, vord,
    out, resid,
    V, mz, raw, H, TFh, TFl, TB, AF, A2, AP, Wh, Wl, S, XF, rb1, rb2, res, R, RX,
    rs_send, rs1_recv, rs2_recv, ag_send, agx_send, ag_recv, agx_recv,
    loc_sem, pair_send, pair_recv, raw_sem, fin_loc, fin_send, fin_recv,
):
    dd, t = lax.axis_index("depth"), lax.axis_index("tile")
    kap, z = dd % 2, dd // 2
    p, c = t % 2, t // 2
    other = 1 - kap
    partner = (z * 2 + other, t)
    reach = (rowb.shape[0] - 1) // 2
    edge = jnp.logical_or(
        jnp.logical_and(kap == 0, z == 3), jnp.logical_and(kap == 1, z == 0)
    )

    def cols(block):
        return pl.ds(pl.multiple_of(block * LANES, LANES), LANES)

    def send(src, dst, s, r, dev):
        return pltpu.make_async_remote_copy(
            src_ref=src, dst_ref=dst, send_sem=s, recv_sem=r, device_id=dev, device_id_type=MESH
        )

    mine = pl.ds(kap * 4, 4)
    theirs = pl.ds(other * 4, 4)

    def block_of(core, lb):
        return core * 4 + lb if lb < 4 else 4 - core

    loads = [
        pltpu.make_async_copy(vol.at[:, :, cols(block_of(kap, lb))], V.at[lb, mine], loc_sem.at[lb])
        for lb in range(5)
    ]
    loads.append(pltpu.make_async_copy(meas.at[:, :, cols(kap * 4 + z)], mz, loc_sem.at[5]))
    for cp in loads:
        cp.start()
    gives = [
        send(vol.at[:, :, cols(block_of(other, lb))], V.at[lb, mine], pair_send.at[lb], pair_recv.at[lb], partner)
        for lb in range(5)
    ]
    for cp in gives:
        cp.start()
    taps = rowb.shape[0]
    j = lax.broadcasted_iota(jnp.int32, (16, rowb.shape[2]), 0)
    pick = jnp.zeros(j.shape, jnp.int32)
    for k in range(steps):
        view = vord[k]
        for d in range(4):
            pick = jnp.where(j == k * 4 + d, kidx[d, view], pick)
    onehot = (pick == lane_of(j.shape)).astype(F32)
    raw[kap] = jnp.zeros(raw.shape[1:], F32)
    for i, bank in enumerate((rowb, colb)):
        for r in range(2):
            raw[kap, 2 * i + r, :, 0:taps] = lax.dot_general(
                onehot, bank[:, r, :], (((1,), (1,)), ((), ())),
                precision=lax.Precision.HIGHEST, preferred_element_type=F32,
            )
    give_raw = send(raw.at[kap], raw.at[kap], raw_sem.at[0], raw_sem.at[1], partner)
    give_raw.start()
    give_raw.wait()
    q = lax.broadcasted_iota(jnp.int32, (LANES, 640), 0)
    l = lax.broadcasted_iota(jnp.int32, (LANES, 640), 1)
    fwd = jnp.logical_and(l < 256, l == jnp.where(q <= reach, reach - q, 256 + reach - q))
    bwd = jnp.logical_and(
        jnp.logical_and(l >= 256, l < 512), l - 256 == jnp.where(q >= reach, q - reach, 256 + q - reach)
    )
    row = l - 512 == 2 * reach - q
    place = jnp.where(fwd | row, 1.0, jnp.where(bwd, -DESCENT, 0.0)).astype(F32)
    H[...] = jnp.dot(
        raw[...].reshape(-1, LANES), place, precision=lax.Precision.HIGHEST, preferred_element_type=F32
    ).reshape(H.shape)

    lane32 = lane_of((32, LANES))
    low = lane32 < 64
    keep = low == (kap == 0)

    def taps_of(src, j, base, start, stop):
        rows = H[src, j, :, start:stop]
        mine = lax.broadcasted_iota(jnp.int32, rows.shape, 0) == base
        return jnp.sum(jnp.where(mine, rows, 0.0), axis=0, keepdims=True)

    def row_mats(k, d):
        base = k * 4 + d % 4
        for r in range(2):
            m = sheared(taps_of(d // 4, r, base, 512, 640), 32)
            m = jnp.where(jnp.logical_and(t == 0, lane32 < reach), 0.0, m)
            m = jnp.where(jnp.logical_and(t == nt - 1, lane32 >= 3 * reach), 0.0, m)
            yield r, m

    def prep_forward(k):
        def plane(d, carry):
            base = k * 4 + d % 4
            for r in range(2):
                hi, lo = split(sheared(taps_of(d // 4, 2 + r, base, 0, 256), LANES))
                at = slice(r * LANES, (r + 1) * LANES)
                TFh[d, 0:128, at] = hi[:, 0:128]
                TFh[d, 128:256, at] = hi[:, 128:256]
                TFl[d, 0:128, at] = lo[:, 0:128]
                TFl[d, 128:256, at] = lo[:, 128:256]
            for r, m in row_mats(k, d):
                AF[d, r * 32 : (r + 1) * 32, :] = m
            return carry

        lax.fori_loop(0, 8, plane, 0)
        for j in range(4):
            m = AF[2 * j : 2 * j + 2].reshape(LANES, LANES).T[0:64]
            hi, lo = split(m)
            A2[0:64, j * LANES : (j + 1) * LANES] = hi
            A2[64:128, j * LANES : (j + 1) * LANES] = lo

    def prep_backward(k):
        def plane(d, carry):
            base = k * 4 + d % 4
            for r in range(2):
                hi, lo = split(sheared(taps_of(d // 4, 2 + r, base, 256, 512), LANES))
                for e in range(2):
                    at = slice(e * 256 + r * LANES, e * 256 + (r + 1) * LANES)
                    TB[d, at, 0:128] = hi[:, e * 128 : (e + 1) * 128]
                    TB[d, at, 128:256] = lo[:, e * 128 : (e + 1) * 128]
            for r, m in row_mats(k, d):
                hi, lo = split(m)
                at = slice(r * 32, (r + 1) * 32)
                both = jnp.where(low, hi.astype(F32), pltpu.roll(lo.astype(F32), 64, 1))
                AP[d, at, 0:128] = both.astype(BF16)
                AP[d, at, 128:256] = hi
            return carry

        lax.fori_loop(0, 8, plane, 0)

    def forward():
        def plane(d, carry):
            v = [V[lb, d] for lb in range(5)]
            rows = []
            for lb in range(4):
                near = jnp.where(low, v[lb + 1], v[(lb + 4) % 5])
                rows.append(jnp.concatenate([v[lb], near], axis=1))
            hi, lo = split(jnp.concatenate(rows, axis=0))
            w = dot(jnp.concatenate([hi, lo], axis=0), TFh[d])
            w = w[0:128] + w[128:256] + dot(hi, TFl[d])
            hi, lo = split(w)
            for lb in range(4):
                for r in range(2):
                    src = (slice(lb * 32, (lb + 1) * 32), slice(r * 128, (r + 1) * 128))
                    dst = (d, slice(r * 32, (r + 1) * 32), slice(lb * 128, (lb + 1) * 128))
                    Wh[dst] = hi[src]
                    Wl[dst] = lo[src]
            return carry

        lax.fori_loop(0, 8, plane, 0)
        s = dot(A2[...], Wh[...].reshape(512, 512))
        s = s[0:64] + s[64:128] + dot(A2[0:64], Wl[...].reshape(512, 512))
        for lb in range(4):
            S[lb] = s[:, lb * 128 : (lb + 1) * 128]

    def backward(k):
        parts = []
        for lb in range(5):
            if lb < 4:
                r = R[lb]
            else:
                r = jnp.where((lane_of((64, LANES)) < 64) == (kap == 0), RX[k], 0.0)
            hi, lo = split(r)
            parts.append(jnp.concatenate([hi, hi, lo, lo], axis=0))
        XF[...] = dot(AP[...].reshape(512, 256), jnp.concatenate(parts, axis=1)).reshape(8, 64, 640)

        def plane(d, carry):
            x = [[XF[d, r * 32 : (r + 1) * 32, lb * 128 : (lb + 1) * 128] for r in range(2)] for lb in range(5)]
            rows = []
            for lb in range(5):
                near = [jnp.where(low, x[(lb + 1) % 5][r], x[(lb + 4) % 5][r]) for r in range(2)]
                rows.append(jnp.concatenate(x[lb] + near, axis=1))
            hi, lo = split(jnp.concatenate(rows, axis=0))
            g = dot(jnp.concatenate([hi, lo], axis=0), TB[d])
            g = g[0:160, 0:128] + (g[0:160, 128:256] + (g[160:320, 0:128] + g[160:320, 128:256]))
            for lb in range(5):
                moved = V[lb, d] + g[lb * 32 : (lb + 1) * 32]
                new = moved - jnp.clip(moved, -SHRINK, SHRINK)
                new = jnp.where(k == steps - 1, moved, new)
                V[lb, d] = new if lb < 4 else jnp.where(keep, new, 0.0)
            return carry

        lax.fori_loop(0, 8, plane, 0)

    def rs_copies():
        slot = p * 4 + z
        n = 0
        cl = c + p - 1
        for hx in range(2):
            for bo in range(4):
                h, b = (p + hx) % 2, (z + bo) % 4
                if hx or bo:
                    rows = pl.ds(pl.multiple_of(((1 - p) * 2 + h) * 16, 16), 16)
                    yield send(S.at[b, rows], rb1.at[slot], rs_send.at[n], rs1_recv.at[slot], (2 * b + kap, 2 * c + h))
                    n += 1
        for h in range(2):
            for bo in range(4):
                b = (z + bo) % 4
                rows = pl.ds(pl.multiple_of((2 * p + h) * 16, 16), 16)
                tile = (2 * cl + 3 * h + nt) % nt
                yield send(S.at[b, rows], rb2.at[slot], rs_send.at[n], rs2_recv.at[slot], (2 * b + kap, tile))
                n += 1

    def rs_wait():
        for hx in range(2):
            for bo in range(4):
                slot = ((p + hx) % 2) * 4 + (z + bo) % 4
                if hx or bo:
                    send(res.at[0], rb1.at[slot], rs_send.at[0], rs1_recv.at[slot], partner).wait_recv()
                send(res.at[0], rb2.at[slot], rs_send.at[0], rs2_recv.at[slot], partner).wait_recv()

    def ag_copies(k, far):
        n = 0
        core = other if far else kap
        cl = c - p
        for kind in range(2):
            for hx in range(2):
                for bo in range(4):
                    h, b = (p + hx) % 2, (z + bo) % 4
                    if kind == 0:
                        tile, g = 2 * c + h, (1 - h) * 2 + p
                        if not (hx or bo or far):
                            continue
                    else:
                        tile, g = (2 * cl + 2 - h + nt) % nt, 2 * h + p
                    rows = pl.ds(pl.multiple_of(g * 16, 16), 16)
                    dev = (2 * b + core, tile)
                    if far:
                        yield send(res.at[kind], RX.at[k, rows], agx_send.at[n], agx_recv.at[k, g], dev)
                    else:
                        yield send(res.at[kind], R.at[z, rows], ag_send.at[n], ag_recv.at[g, z], dev)
                    n += 1

    def ag_wait(k):
        for g in range(4):
            for b in range(4):
                @pl.when(jnp.logical_or(g != 2 - p, b != z))
                def _():
                    send(res.at[0], R.at[b, g * 16 : g * 16 + 16], ag_send.at[0], ag_recv.at[g, b], partner).wait_recv()
            send(res.at[0], RX.at[k, g * 16 : g * 16 + 16], ag_send.at[0], agx_recv.at[k, g], partner).wait_recv()

    prep_forward(0)
    for cp in loads:
        cp.wait()
    for cp in gives:
        cp.wait()
    for d in range(8):
        V[4, d] = jnp.where(keep, V[4, d], 0.0)

    def step(k, carry):
        forward()
        S[z, 16:48] = S[z, 16:48] - mz[k]
        for cp in rs_copies():
            cp.start()
        prep_backward(k)
        rs_wait()
        own = pl.ds(pl.multiple_of((2 - p) * 16, 16), 16)
        total1 = S[z, own]
        total2 = rb2[p * 4 + z]
        for hx in range(2):
            for bo in range(4):
                if hx or bo:
                    slot = ((p + hx) % 2) * 4 + (z + bo) % 4
                    total1 = total1 + rb1[slot]
                    total2 = total2 + rb2[slot]
        res[0] = total1
        res[1] = total2
        for cp in ag_copies(k, False):
            cp.start()

        @pl.when(edge)
        def _():
            for cp in ag_copies(k, True):
                cp.start()

        R[z, own] = total1
        prep_forward(jnp.minimum(k + 1, steps - 1))
        for cp in rs_copies():
            cp.wait_send()
        ag_wait(k)
        backward(k)
        for cp in ag_copies(k, False):
            cp.wait_send()

        @pl.when(edge)
        def _():
            for cp in ag_copies(k, True):
                cp.wait_send()

        return carry

    lax.fori_loop(0, steps, step, 0)

    ends = []
    for lb in range(4):
        here = cols(kap * 4 + lb)
        ends.append(pltpu.make_async_copy(V.at[lb, mine], out.at[:, :, here], fin_loc.at[lb]))
        ends.append(pltpu.make_async_copy(R.at[lb, 16:48], resid.at[:, here], fin_loc.at[4 + lb]))
        ends.append(send(V.at[lb, theirs], out.at[:, :, here], fin_send.at[lb], fin_recv.at[lb], partner))
        ends.append(send(R.at[lb, 16:48], resid.at[:, here], fin_send.at[4 + lb], fin_recv.at[4 + lb], partner))
    for cp in ends:
        cp.start()
    for cp in ends:
        cp.wait()


def solution(mesh):
    nt = mesh.shape["tile"]

    def per_device(volume, measured, row_bank, col_bank, kernel_index, view_order):
        steps, rows, width = measured.shape
        vm, dma = pltpu.VMEM, pltpu.SemaphoreType.DMA
        anywhere = pl.BlockSpec(memory_space=pl.ANY)
        moved, resid = pl.pallas_call(
            functools.partial(kernel, nt, steps),
            name="ista",
            out_shape=(
                jax.ShapeDtypeStruct(volume.shape, F32),
                jax.ShapeDtypeStruct((rows, width), F32),
            ),
            in_specs=[
                anywhere,
                anywhere,
                pl.BlockSpec(memory_space=vm),
                pl.BlockSpec(memory_space=vm),
                pl.BlockSpec(memory_space=pltpu.SMEM),
                pl.BlockSpec(memory_space=pltpu.SMEM),
            ],
            out_specs=(anywhere, anywhere),
            scratch_shapes=[
                vm((5, 8, rows, LANES), F32),
                vm((steps, rows, LANES), F32),
                vm((2, 4, 16, LANES), F32),
                vm((2, 4, 16, 640), F32),
                vm((8, 256, 256), BF16),
                vm((8, 256, 256), BF16),
                vm((8, 512, 256), BF16),
                vm((8, 64, LANES), F32),
                vm((128, 512), BF16),
                vm((8, 64, 256), BF16),
                vm((8, 64, 512), BF16),
                vm((8, 64, 512), BF16),
                vm((4, 64, LANES), F32),
                vm((8, 64, 640), F32),
                vm((8, 16, LANES), F32),
                vm((8, 16, LANES), F32),
                vm((2, 16, LANES), F32),
                vm((4, 64, LANES), F32),
                vm((steps, 64, LANES), F32),
                dma((15,)),
                dma((8,)),
                dma((8,)),
                dma((15,)),
                dma((16,)),
                dma((4, 4)),
                dma((steps, 4)),
                dma((6,)),
                dma((5,)),
                dma((5,)),
                dma((2,)),
                dma((8,)),
                dma((8,)),
                dma((8,)),
            ],
            compiler_params=pltpu.CompilerParams(has_side_effects=True, vmem_limit_bytes=60 * 1024 * 1024),
        )(volume, measured, row_bank.T, col_bank.T, kernel_index.T, view_order)
        return moved - jnp.clip(moved, -SHRINK, SHRINK), resid

    return jax.shard_map(
        per_device,
        mesh=mesh,
        in_specs=(P("depth", "tile", None), P(None, "tile", None), P(), P(), P(None, "depth"), P()),
        out_specs=(P("depth", "tile", None), P("tile", None)),
        check_vma=False,
    )
```

```python
import functools

import jax
import jax.numpy as jnp
from jax import lax
from jax.experimental import pallas as pl
from jax.experimental.pallas import tpu as pltpu
from jax.sharding import PartitionSpec as P

MESH = pl.DeviceIdType.MESH
DESCENT = 0.5
SHRINK = 0.1
LANES = 128
F32, BF16 = jnp.float32, jnp.bfloat16


def split(x):
    hi = x.astype(BF16)
    return hi, (x - hi.astype(F32)).astype(BF16)


def dot(a, b):
    return jnp.dot(a, b, preferred_element_type=F32)


def lane_of(shape):
    return lax.broadcasted_iota(jnp.int32, shape, len(shape) - 1)


def sheared(row, rows):
    wide = jnp.broadcast_to(row, (rows, row.shape[1]))
    return pltpu.roll(wide, 0, 1, stride=1, stride_axis=0)


def kernel(
    nt, steps,
    vol, meas, rowb, colb, kidx, vord,
    out, resid,
    V, mz, raw, H, TFh, TFl, TB, AF, A2, AP, Wh, Wl, S, XF, rb1, rb2, res1, res2, R, RX,
    rs_send, rs1_recv, rs2_recv, ag1_send, ag2_send, agx1_send, agx2_send,
    ag1_recv, ag2_recv, agx1_recv, agx2_recv, loc_sem, pair_send, pair_recv, raw_sem, fin_loc, fin_send, fin_recv,
):
    dd, t = lax.axis_index("depth"), lax.axis_index("tile")
    kap, z = dd % 2, dd // 2
    p, c = t % 2, t // 2
    other = 1 - kap
    partner = (z * 2 + other, t)
    reach = (rowb.shape[0] - 1) // 2
    low2 = 2 * (c + p - 1)
    own2 = 2 * (c - p)
    inner = jnp.logical_or(z == 1, z == 2)
    block2 = 2 * p + z - 1
    edge1 = z == 3 - 3 * kap
    edge2 = jnp.logical_and(inner, block2 == 3 - 3 * kap)

    def wrapped(tile):
        return (tile + 2 * nt) % nt

    def owner2(b, core):
        return ((1 + b % 2) * 2 + core, wrapped(low2 + 3 * (b // 2)))

    def around():
        for hx in range(2):
            for bo in range(4):
                if hx or bo:
                    yield (p + hx) % 2, (z + bo) % 4

    def members2():
        for h in range(2):
            for bo in range(4):
                yield wrapped(own2 + 2 - h), h, (z + bo) % 4

    def cols(block):
        return pl.ds(pl.multiple_of(block * LANES, LANES), LANES)

    def send(src, dst, s, r, dev):
        return pltpu.make_async_remote_copy(
            src_ref=src, dst_ref=dst, send_sem=s, recv_sem=r, device_id=dev, device_id_type=MESH
        )

    mine = pl.ds(kap * 4, 4)
    theirs = pl.ds(other * 4, 4)

    def block_of(core, lb):
        return core * 4 + lb if lb < 4 else 4 - core

    loads = [
        pltpu.make_async_copy(vol.at[:, :, cols(block_of(kap, lb))], V.at[lb, mine], loc_sem.at[lb])
        for lb in range(5)
    ]
    loads.append(pltpu.make_async_copy(meas.at[:, :, cols(kap * 4 + z)], mz, loc_sem.at[5]))
    for cp in loads:
        cp.start()
    gives = [
        send(vol.at[:, :, cols(block_of(other, lb))], V.at[lb, mine], pair_send.at[lb], pair_recv.at[lb], partner)
        for lb in range(5)
    ]
    barrier = pltpu.get_barrier_semaphore()

    def greet(dev):
        pl.semaphore_signal(barrier, inc=1, device_id=dev, device_id_type=MESH)

    greet(partner)
    for h, b in around():
        greet((2 * b + kap, 2 * c + h))
    for b in range(4):
        greet(owner2(b, kap))
    far1, far2 = 3 * kap, 3 * kap
    for h in range(2):
        greet((2 * far1 + other, 2 * c + h))
    greet(owner2(far2, other))

    @pl.when(edge1)
    def _():
        for h in range(2):
            for b in range(4):
                greet((2 * b + other, 2 * c + h))

    @pl.when(inner)
    def _():
        for tile, h, b in members2():
            greet((2 * b + kap, tile))

    @pl.when(edge2)
    def _():
        for tile, h, b in members2():
            greet((2 * b + other, tile))

    n_greets = 1 + 7 + 4 + 3 + 8 * (edge1.astype(jnp.int32) + inner.astype(jnp.int32) + edge2.astype(jnp.int32))

    taps = rowb.shape[0]
    j = lax.broadcasted_iota(jnp.int32, (16, rowb.shape[2]), 0)
    pick = jnp.zeros(j.shape, jnp.int32)
    for k in range(steps):
        view = vord[k]
        for d in range(4):
            pick = jnp.where(j == k * 4 + d, kidx[d, view], pick)
    onehot = (pick == lane_of(j.shape)).astype(F32)
    raw[kap] = jnp.zeros(raw.shape[1:], F32)
    for i, bank in enumerate((rowb, colb)):
        for r in range(2):
            raw[kap, 2 * i + r, :, 0:taps] = lax.dot_general(
                onehot, bank[:, r, :], (((1,), (1,)), ((), ())),
                precision=lax.Precision.HIGHEST, preferred_element_type=F32,
            )
    give_raw = send(raw.at[kap], raw.at[kap], raw_sem.at[0], raw_sem.at[1], partner)
    take_raw = send(raw.at[other], raw.at[other], raw_sem.at[0], raw_sem.at[1], partner)
    q = lax.broadcasted_iota(jnp.int32, (LANES, 640), 0)
    l = lax.broadcasted_iota(jnp.int32, (LANES, 640), 1)
    fwd = jnp.logical_and(l < 256, l == jnp.where(q <= reach, reach - q, 256 + reach - q))
    bwd = jnp.logical_and(
        jnp.logical_and(l >= 256, l < 512), l - 256 == jnp.where(q >= reach, q - reach, 256 + q - reach)
    )
    row = l - 512 == 2 * reach - q
    place = jnp.where(fwd | row, 1.0, jnp.where(bwd, -DESCENT, 0.0)).astype(F32)

    def place_taps(core):
        H[core] = jnp.dot(
            raw[core].reshape(-1, LANES), place, precision=lax.Precision.HIGHEST, preferred_element_type=F32
        ).reshape(H.shape[1:])

    lane32 = lane_of((32, LANES))
    low = lane32 < 64
    keep = low == (kap == 0)

    def taps_of(src, j, base, start, stop):
        rows = H[src, j, :, start:stop]
        mine = lax.broadcasted_iota(jnp.int32, rows.shape, 0) == base
        return jnp.sum(jnp.where(mine, rows, 0.0), axis=0, keepdims=True)

    def row_mats(k, d):
        base = k * 4 + d % 4
        for r in range(2):
            m = sheared(taps_of(d // 4, r, base, 512, 640), 32)
            m = jnp.where(jnp.logical_and(t == 0, lane32 < reach), 0.0, m)
            m = jnp.where(jnp.logical_and(t == nt - 1, lane32 >= 3 * reach), 0.0, m)
            yield r, m

    def prep_forward(k, core):
        def plane(j, carry):
            d = core * 4 + j
            base = k * 4 + d % 4
            for r in range(2):
                hi, lo = split(sheared(taps_of(d // 4, 2 + r, base, 0, 256), LANES))
                at = slice(r * LANES, (r + 1) * LANES)
                TFh[d, 0:128, at] = hi[:, 0:128]
                TFh[d, 128:256, at] = hi[:, 128:256]
                TFl[d, 0:128, at] = lo[:, 0:128]
                TFl[d, 128:256, at] = lo[:, 128:256]
            for r, m in row_mats(k, d):
                AF[d, r * 32 : (r + 1) * 32, :] = m
            return carry

        lax.fori_loop(0, 4, plane, 0)
        for j in range(2):
            m = AF[pl.ds(core * 4 + 2 * j, 2)].reshape(LANES, LANES).T[0:64]
            hi, lo = split(m)
            A2[0:64, cols(core * 2 + j)] = hi
            A2[64:128, cols(core * 2 + j)] = lo

    def prep_backward(k):
        def plane(d, carry):
            base = k * 4 + d % 4
            for r in range(2):
                hi, lo = split(sheared(taps_of(d // 4, 2 + r, base, 256, 512), LANES))
                for e in range(2):
                    at = slice(e * 256 + r * LANES, e * 256 + (r + 1) * LANES)
                    TB[d, at, 0:128] = hi[:, e * 128 : (e + 1) * 128]
                    TB[d, at, 128:256] = lo[:, e * 128 : (e + 1) * 128]
            for r, m in row_mats(k, d):
                hi, lo = split(m)
                at = slice(r * 32, (r + 1) * 32)
                both = jnp.where(low, hi.astype(F32), pltpu.roll(lo.astype(F32), 64, 1))
                AP[d, at, 0:128] = both.astype(BF16)
                AP[d, at, 128:256] = hi
            return carry

        lax.fori_loop(0, 8, plane, 0)

    def forward_planes(core):
        def plane(j, carry):
            d = core * 4 + j
            v = [V[lb, d] for lb in range(5)]
            rows = []
            for lb in range(4):
                near = jnp.where(low, v[lb + 1], v[(lb + 4) % 5])
                rows.append(jnp.concatenate([v[lb], near], axis=1))
            hi, lo = split(jnp.concatenate(rows, axis=0))
            w = dot(jnp.concatenate([hi, lo], axis=0), TFh[d])
            w = w[0:128] + w[128:256] + dot(hi, TFl[d])
            hi, lo = split(w)
            for lb in range(4):
                for r in range(2):
                    src = (slice(lb * 32, (lb + 1) * 32), slice(r * 128, (r + 1) * 128))
                    dst = (d, slice(r * 32, (r + 1) * 32), slice(lb * 128, (lb + 1) * 128))
                    Wh[dst] = hi[src]
                    Wl[dst] = lo[src]
            return carry

        lax.fori_loop(0, 4, plane, 0)

    def forward_rows():
        s = dot(A2[...], Wh[...].reshape(512, 512))
        s = s[0:64] + s[64:128] + dot(A2[0:64], Wl[...].reshape(512, 512))
        for lb in range(4):
            S[lb] = s[:, lb * 128 : (lb + 1) * 128]

    def backward_rows(k):
        parts = []
        for lb in range(5):
            if lb < 4:
                r = R[lb]
            else:
                r = jnp.where((lane_of((64, LANES)) < 64) == (kap == 0), RX[k], 0.0)
            hi, lo = split(r)
            parts.append(jnp.concatenate([hi, hi, lo, lo], axis=0))
        XF[...] = dot(AP[...].reshape(512, 256), jnp.concatenate(parts, axis=1)).reshape(8, 64, 640)

    def backward_planes(k, core):
        def plane(j, carry):
            d = core * 4 + j
            x = [[XF[d, r * 32 : (r + 1) * 32, lb * 128 : (lb + 1) * 128] for r in range(2)] for lb in range(5)]
            rows = []
            for lb in range(5):
                near = [jnp.where(low, x[(lb + 1) % 5][r], x[(lb + 4) % 5][r]) for r in range(2)]
                rows.append(jnp.concatenate(x[lb] + near, axis=1))
            hi, lo = split(jnp.concatenate(rows, axis=0))
            g = dot(jnp.concatenate([hi, lo], axis=0), TB[d])
            g = g[0:160, 0:128] + (g[0:160, 128:256] + (g[160:320, 0:128] + g[160:320, 128:256]))
            for lb in range(5):
                moved = V[lb, d] + g[lb * 32 : (lb + 1) * 32]
                new = moved - jnp.clip(moved, -SHRINK, SHRINK)
                new = jnp.where(k == steps - 1, moved, new)
                V[lb, d] = new if lb < 4 else jnp.where(keep, new, 0.0)
            return carry

        lax.fori_loop(0, 4, plane, 0)

    def rows16(g):
        return pl.ds(pl.multiple_of(g * 16, 16), 16)

    slot = p * 4 + z
    half1 = pl.ds(pl.multiple_of((1 - p) * 32, 32), 32)
    half2 = pl.ds(pl.multiple_of(p * 32, 32), 32)
    own = rows16(2 - p)

    def rs_copies():
        n = 0
        for b in range(4):
            yield send(S.at[b, half2], rb2.at[slot], rs_send.at[n], rs2_recv.at[slot], owner2(b, kap))
            n += 1
        for h, b in around():
            src = S.at[b, rows16((1 - p) * 2 + h)]
            yield send(src, rb1.at[slot], rs_send.at[n], rs1_recv.at[slot], (2 * b + kap, 2 * c + h))
            n += 1

    def ag1_copies():
        for n, (h, b) in enumerate(around()):
            g = (1 - h) * 2 + p
            yield send(res1, R.at[z, rows16(g)], ag1_send.at[n], ag1_recv.at[p, z], (2 * b + kap, 2 * c + h))

    def agx1_copies(k):
        for h in range(2):
            for b in range(4):
                g = (1 - h) * 2 + p
                n = h * 4 + b
                yield send(res1, RX.at[k, rows16(g)], agx1_send.at[n], agx1_recv.at[k, p], (2 * b + other, 2 * c + h))

    def ag2_copies():
        for n, (tile, h, b) in enumerate(members2()):
            dst = R.at[block2, pl.ds(pl.multiple_of(h * 32, 32), 32)]
            yield send(res2, dst, ag2_send.at[n], ag2_recv.at[block2], (2 * b + kap, tile))

    def agx2_copies(k):
        for n, (tile, h, b) in enumerate(members2()):
            dst = RX.at[k, pl.ds(pl.multiple_of(h * 32, 32), 32)]
            yield send(res2, dst, agx2_send.at[n], agx2_recv.at[k], (2 * b + other, tile))

    def came(dst, sem):
        send(dst, dst, rs_send.at[0], sem, partner).wait_recv()

    def masked_edge(core):
        for j in range(4):
            V[4, core * 4 + j] = jnp.where(keep, V[4, core * 4 + j], 0.0)

    place_taps(kap)
    prep_forward(0, kap)
    for cp in loads:
        cp.wait()
    masked_edge(kap)
    pl.semaphore_wait(barrier, n_greets)
    give_raw.start()
    for cp in gives:
        cp.start()
    forward_planes(kap)
    take_raw.wait_recv()
    place_taps(other)
    prep_forward(0, other)
    for lb in range(5):
        came(V.at[lb, theirs], pair_recv.at[lb])
    masked_edge(other)
    forward_planes(other)
    forward_rows()
    give_raw.wait_send()
    for cp in gives:
        cp.wait_send()

    def finals():
        for lb in range(4):
            here = cols(kap * 4 + lb)
            yield send(V.at[lb, theirs], out.at[:, :, here], fin_send.at[lb], fin_recv.at[lb], partner)

    def finals_resid():
        for lb in range(4):
            here = cols(kap * 4 + lb)
            yield send(R.at[lb, 16:48], resid.at[:, here], fin_send.at[4 + lb], fin_recv.at[4 + lb], partner)
            yield pltpu.make_async_copy(R.at[lb, 16:48], resid.at[:, here], fin_loc.at[4 + lb])

    def finals_here():
        for lb in range(4):
            yield pltpu.make_async_copy(V.at[lb, mine], out.at[:, :, cols(kap * 4 + lb)], fin_loc.at[lb])

    def step(k, carry):
        S[z, 16:48] = S[z, 16:48] - mz[k]
        for cp in rs_copies():
            cp.start()
        prep_backward(k)

        @pl.when(inner)
        def _():
            total = jnp.zeros((32, LANES), F32)
            for q in range(8):
                came(rb2.at[q], rs2_recv.at[q])
                total = total + rb2[q]
            res2[...] = total
            for cp in ag2_copies():
                cp.start()

        @pl.when(edge2)
        def _():
            for cp in agx2_copies(k):
                cp.start()

        total = S[z, own]
        for h, b in around():
            came(rb1.at[h * 4 + b], rs1_recv.at[h * 4 + b])
            total = total + rb1[h * 4 + b]
        res1[...] = total
        for cp in ag1_copies():
            cp.start()

        @pl.when(edge1)
        def _():
            for cp in agx1_copies(k):
                cp.start()

        R[z, own] = total
        nxt = jnp.minimum(k + 1, steps - 1)
        prep_forward(nxt, kap)
        prep_forward(nxt, other)
        for cp in rs_copies():
            cp.wait_send()
        for h, b in around():
            came(R.at[b, rows16((1 - p) * 2 + h)], ag1_recv.at[h, b])
        for b in range(4):
            came(R.at[b, half2], ag2_recv.at[b])
        for h in range(2):
            came(RX.at[k, rows16((1 - p) * 2 + h)], agx1_recv.at[k, h])
        came(RX.at[k, half2], agx2_recv.at[k])
        last = k == steps - 1

        @pl.when(last)
        def _():
            for cp in finals_resid():
                cp.start()

        backward_rows(k)
        backward_planes(k, other)

        @pl.when(last)
        def _():
            for cp in finals():
                cp.start()

        backward_planes(k, kap)
        for cp in ag1_copies():
            cp.wait_send()

        @pl.when(edge1)
        def _():
            for cp in agx1_copies(k):
                cp.wait_send()

        @pl.when(inner)
        def _():
            for cp in ag2_copies():
                cp.wait_send()

        @pl.when(edge2)
        def _():
            for cp in agx2_copies(k):
                cp.wait_send()

        @pl.when(jnp.logical_not(last))
        def _():
            forward_planes(kap)
            forward_planes(other)
            forward_rows()

        return carry

    lax.fori_loop(0, steps, step, 0)
    for cp in finals_here():
        cp.start()
    for cp in (*finals_here(), *finals_resid(), *finals()):
        cp.wait()


def solution(mesh):
    nt = mesh.shape["tile"]

    def per_device(volume, measured, row_bank, col_bank, kernel_index, view_order):
        steps, rows, width = measured.shape
        vm, dma = pltpu.VMEM, pltpu.SemaphoreType.DMA
        anywhere = pl.BlockSpec(memory_space=pl.ANY)
        moved, resid = pl.pallas_call(
            functools.partial(kernel, nt, steps),
            name="ista",
            out_shape=(
                jax.ShapeDtypeStruct(volume.shape, F32),
                jax.ShapeDtypeStruct((rows, width), F32),
            ),
            in_specs=[
                pl.BlockSpec(memory_space=pltpu.HBM),
                pl.BlockSpec(memory_space=pltpu.HBM),
                pl.BlockSpec(memory_space=vm),
                pl.BlockSpec(memory_space=vm),
                pl.BlockSpec(memory_space=pltpu.SMEM),
                pl.BlockSpec(memory_space=pltpu.SMEM),
            ],
            out_specs=(anywhere, anywhere),
            scratch_shapes=[
                vm((5, 8, rows, LANES), F32),
                vm((steps, rows, LANES), F32),
                vm((2, 4, 16, LANES), F32),
                vm((2, 4, 16, 640), F32),
                vm((8, 256, 256), BF16),
                vm((8, 256, 256), BF16),
                vm((8, 512, 256), BF16),
                vm((8, 64, LANES), F32),
                vm((128, 512), BF16),
                vm((8, 64, 256), BF16),
                vm((8, 64, 512), BF16),
                vm((8, 64, 512), BF16),
                vm((4, 64, LANES), F32),
                vm((8, 64, 640), F32),
                vm((8, 16, LANES), F32),
                vm((8, 32, LANES), F32),
                vm((16, LANES), F32),
                vm((32, LANES), F32),
                vm((4, 64, LANES), F32),
                vm((steps, 64, LANES), F32),
                dma((11,)),
                dma((8,)),
                dma((8,)),
                dma((7,)),
                dma((8,)),
                dma((8,)),
                dma((8,)),
                dma((2, 4)),
                dma((4,)),
                dma((steps, 2)),
                dma((steps,)),
                dma((6,)),
                dma((5,)),
                dma((5,)),
                dma((2,)),
                dma((8,)),
                dma((8,)),
                dma((8,)),
            ],
            compiler_params=pltpu.CompilerParams(
                collective_id=0, has_side_effects=True, vmem_limit_bytes=60 * 1024 * 1024
            ),
        )(volume, measured, row_bank.T, col_bank.T, kernel_index.T, view_order)
        return moved - jnp.clip(moved, -SHRINK, SHRINK), resid

    return jax.shard_map(
        per_device,
        mesh=mesh,
        in_specs=(P("depth", "tile", None), P(None, "tile", None), P(), P(), P(None, "depth"), P()),
        out_specs=(P("depth", "tile", None), P("tile", None)),
        check_vma=False,
    )
```

```python
import functools

import jax
import jax.numpy as jnp
from jax import lax
from jax.experimental import pallas as pl
from jax.experimental.pallas import tpu as pltpu
from jax.sharding import PartitionSpec as P

MESH = pl.DeviceIdType.MESH
DESCENT = 0.5
SHRINK = 0.1
LANES = 128
F32, BF16 = jnp.float32, jnp.bfloat16


def split(x):
    hi = x.astype(BF16)
    return hi, (x - hi.astype(F32)).astype(BF16)


def dot(a, b):
    return jnp.dot(a, b, preferred_element_type=F32)


def lane_of(shape):
    return lax.broadcasted_iota(jnp.int32, shape, len(shape) - 1)


def sheared(row, rows):
    wide = jnp.broadcast_to(row, (rows, row.shape[1]))
    return pltpu.roll(wide, 0, 1, stride=1, stride_axis=0)


def kernel(
    nt, steps,
    vol, meas, rowb, colb, kidx, vord,
    out, resid,
    V, mz, raw, H, TFh, TFl, TB, AF, A2, AP, Wh, Wl, S, XF, rb1, rb2, res1, res2, ex1, ex2, R, px1, px2,
    rs_send, rs1_recv, rs2_recv, ag1_send, ag2_send, agx1_send, agx2_send,
    ag1_recv, ag2_recv, agx1_recv, agx2_recv, loc_sem, pair_send, pair_recv, raw_sem, fin_loc, fin_send, fin_recv,
):
    dd, t = lax.axis_index("depth"), lax.axis_index("tile")
    kap, z = dd % 2, dd // 2
    p, c = t % 2, t // 2
    other = 1 - kap
    partner = (z * 2 + other, t)
    reach = (rowb.shape[0] - 1) // 2
    low2 = 2 * (c + p - 1)
    own2 = 2 * (c - p)
    inner = jnp.logical_or(z == 1, z == 2)
    block2 = 2 * p + z - 1
    edge1 = z == 3 - 3 * kap
    edge2 = jnp.logical_and(inner, block2 == 3 - 3 * kap)

    def wrapped(tile):
        return (tile + 2 * nt) % nt

    def owner2(b, core):
        return ((1 + b % 2) * 2 + core, wrapped(low2 + 3 * (b // 2)))

    def around():
        for hx in (1, 0):
            for bo in (2, 1, 3, 0):
                if hx or bo:
                    yield (p + hx) % 2, (z + bo) % 4

    def members2():
        for bo in (2, 3, 1, 0):
            for hx in (1, 0):
                h = (p + hx) % 2
                yield wrapped(own2 + 2 - h), h, (z + bo) % 4

    def cols(block):
        return pl.ds(pl.multiple_of(block * LANES, LANES), LANES)

    def send(src, dst, s, r, dev):
        return pltpu.make_async_remote_copy(
            src_ref=src, dst_ref=dst, send_sem=s, recv_sem=r, device_id=dev, device_id_type=MESH
        )

    mine = pl.ds(kap * 4, 4)
    theirs = pl.ds(other * 4, 4)

    def block_of(core, lb):
        return core * 4 + lb if lb < 4 else 4 - core

    loads = [
        pltpu.make_async_copy(vol.at[:, :, cols(block_of(kap, lb))], V.at[lb, mine], loc_sem.at[lb])
        for lb in range(5)
    ]
    loads.append(pltpu.make_async_copy(meas.at[:, :, cols(kap * 4 + z)], mz, loc_sem.at[5]))
    for cp in loads:
        cp.start()
    gives = [
        send(vol.at[:, :, cols(block_of(other, lb))], V.at[lb, mine], pair_send.at[lb], pair_recv.at[lb], partner)
        for lb in range(5)
    ]
    barrier = pltpu.get_barrier_semaphore()

    def greet(dev):
        pl.semaphore_signal(barrier, inc=1, device_id=dev, device_id_type=MESH)

    greet(partner)
    for h, b in around():
        greet((2 * b + kap, 2 * c + h))
    for b in range(4):
        greet(owner2(b, kap))
    far1, far2 = 3 * kap, 3 * kap
    for h in range(2):
        greet((2 * far1 + other, 2 * c + h))
    greet(owner2(far2, other))

    @pl.when(edge1)
    def _():
        for h in range(2):
            for b in range(4):
                greet((2 * b + other, 2 * c + h))

    @pl.when(inner)
    def _():
        for tile, h, b in members2():
            greet((2 * b + kap, tile))

    @pl.when(edge2)
    def _():
        for tile, h, b in members2():
            greet((2 * b + other, tile))

    n_greets = 1 + 7 + 4 + 3 + 8 * (edge1.astype(jnp.int32) + inner.astype(jnp.int32) + edge2.astype(jnp.int32))

    taps = rowb.shape[0]
    j = lax.broadcasted_iota(jnp.int32, (16, rowb.shape[2]), 0)
    pick = jnp.zeros(j.shape, jnp.int32)
    for k in range(steps):
        view = vord[k]
        for d in range(4):
            pick = jnp.where(j == k * 4 + d, kidx[d, view], pick)
    onehot = (pick == lane_of(j.shape)).astype(F32)
    raw[kap] = jnp.zeros(raw.shape[1:], F32)
    for i, bank in enumerate((rowb, colb)):
        for r in range(2):
            raw[kap, 2 * i + r, :, 0:taps] = lax.dot_general(
                onehot, bank[:, r, :], (((1,), (1,)), ((), ())),
                precision=lax.Precision.HIGHEST, preferred_element_type=F32,
            )
    give_raw = send(raw.at[kap], raw.at[kap], raw_sem.at[0], raw_sem.at[1], partner)
    take_raw = send(raw.at[other], raw.at[other], raw_sem.at[0], raw_sem.at[1], partner)
    q = lax.broadcasted_iota(jnp.int32, (LANES, 640), 0)
    l = lax.broadcasted_iota(jnp.int32, (LANES, 640), 1)
    fwd = jnp.logical_and(l < 256, l == jnp.where(q <= reach, reach - q, 256 + reach - q))
    bwd = jnp.logical_and(
        jnp.logical_and(l >= 256, l < 512), l - 256 == jnp.where(q >= reach, q - reach, 256 + q - reach)
    )
    row = l - 512 == 2 * reach - q
    place = jnp.where(fwd | row, 1.0, jnp.where(bwd, -DESCENT, 0.0)).astype(F32)

    def place_taps(core):
        H[core] = jnp.dot(
            raw[core].reshape(-1, LANES), place, precision=lax.Precision.HIGHEST, preferred_element_type=F32
        ).reshape(H.shape[1:])

    lane32 = lane_of((32, LANES))
    low = lane32 < 64
    keep = low == (kap == 0)

    def taps_of(src, j, base, start, stop):
        rows = H[src, j, :, start:stop]
        mine = lax.broadcasted_iota(jnp.int32, rows.shape, 0) == base
        return jnp.sum(jnp.where(mine, rows, 0.0), axis=0, keepdims=True)

    def row_mats(k, d):
        base = k * 4 + d % 4
        for r in range(2):
            m = sheared(taps_of(d // 4, r, base, 512, 640), 32)
            m = jnp.where(jnp.logical_and(t == 0, lane32 < reach), 0.0, m)
            m = jnp.where(jnp.logical_and(t == nt - 1, lane32 >= 3 * reach), 0.0, m)
            yield r, m

    def prep_forward(k, core):
        def plane(j, carry):
            d = core * 4 + j
            base = k * 4 + d % 4
            for r in range(2):
                hi, lo = split(sheared(taps_of(d // 4, 2 + r, base, 0, 256), LANES))
                at = slice(r * LANES, (r + 1) * LANES)
                TFh[d, 0:128, at] = hi[:, 0:128]
                TFh[d, 128:256, at] = hi[:, 128:256]
                TFl[d, 0:128, at] = lo[:, 0:128]
                TFl[d, 128:256, at] = lo[:, 128:256]
            for r, m in row_mats(k, d):
                AF[d, r * 32 : (r + 1) * 32, :] = m
            return carry

        lax.fori_loop(0, 4, plane, 0, unroll=True)
        for j in range(2):
            m = AF[pl.ds(core * 4 + 2 * j, 2)].reshape(LANES, LANES).T[0:64]
            hi, lo = split(m)
            A2[0:64, cols(core * 2 + j)] = hi
            A2[64:128, cols(core * 2 + j)] = lo

    def prep_backward(k):
        def plane(d, carry):
            base = k * 4 + d % 4
            for r in range(2):
                hi, lo = split(sheared(taps_of(d // 4, 2 + r, base, 256, 512), LANES))
                for e in range(2):
                    at = slice(e * 256 + r * LANES, e * 256 + (r + 1) * LANES)
                    TB[d, at, 0:128] = hi[:, e * 128 : (e + 1) * 128]
                    TB[d, at, 128:256] = lo[:, e * 128 : (e + 1) * 128]
            for r, m in row_mats(k, d):
                hi, lo = split(m)
                at = slice(r * 32, (r + 1) * 32)
                both = jnp.where(low, hi.astype(F32), pltpu.roll(lo.astype(F32), 64, 1))
                AP[d, at, 0:128] = both.astype(BF16)
                AP[d, at, 128:256] = hi
            return carry

        lax.fori_loop(0, 8, plane, 0)

    def forward_planes(core):
        def plane(j, carry):
            d = core * 4 + j
            v = [split(V[lb, d]) for lb in range(5)]
            hi, lo = (
                jnp.concatenate(
                    [
                        jnp.concatenate([v[lb][i], jnp.where(low, v[lb + 1][i], v[(lb + 4) % 5][i])], axis=1)
                        for lb in range(4)
                    ],
                    axis=0,
                )
                for i in range(2)
            )
            w = dot(jnp.concatenate([hi, lo], axis=0), TFh[d])
            w = w[0:128] + w[128:256] + dot(hi, TFl[d])
            hi, lo = split(w)
            for lb in range(4):
                for r in range(2):
                    src = (slice(lb * 32, (lb + 1) * 32), slice(r * 128, (r + 1) * 128))
                    dst = (d, slice(r * 32, (r + 1) * 32), slice(lb * 128, (lb + 1) * 128))
                    Wh[dst] = hi[src]
                    Wl[dst] = lo[src]
            return carry

        lax.fori_loop(0, 4, plane, 0, unroll=True)

    def forward_rows(k):
        for pair in range(2):
            at = slice(pair * 256, (pair + 1) * 256)
            s = dot(A2[...], Wh[:, :, at].reshape(512, 256))
            s = s[0:64] + s[64:128] + dot(A2[0:64], Wl[:, :, at].reshape(512, 256))
            for i in range(2):
                b = 2 * pair + i
                block = s[:, i * 128 : (i + 1) * 128]
                S[b, 0:16] = block[0:16]
                S[b, 16:48] = block[16:48] - jnp.where(z == b, mz[k], 0.0)
                S[b, 48:64] = block[48:64]
            for i in range(2):
                for cp in rs_copies(2 * pair + i):
                    cp("start")

    def backward_rows(k):
        ap = AP[...].reshape(512, 256)
        for pair in range(3):
            parts = []
            for lb in range(2 * pair, min(2 * pair + 2, 5)):
                if lb < 4:
                    ag_arrived(lb)
                    r = R[lb]
                else:
                    r = edge_rows(k)
                hi, lo = split(r)
                parts.append(jnp.concatenate([hi, hi, lo, lo], axis=0))
            x = dot(ap, jnp.concatenate(parts, axis=1)).reshape(8, 64, 128 * len(parts))
            hi, lo = split(x)
            at = slice(pair * 256, pair * 256 + 128 * len(parts))
            XF[0, :, :, at] = hi
            XF[1, :, :, at] = lo

    def backward_planes(k, core):
        def plane(j, carry):
            d = core * 4 + j
            rows = []
            for i in range(2):
                x = [
                    [XF[i, d, r * 32 : (r + 1) * 32, lb * 128 : (lb + 1) * 128] for r in range(2)] for lb in range(5)
                ]
                for lb in range(5):
                    near = [jnp.where(low, x[(lb + 1) % 5][r], x[(lb + 4) % 5][r]) for r in range(2)]
                    rows.append(jnp.concatenate(x[lb] + near, axis=1))
            g = dot(jnp.concatenate(rows, axis=0), TB[d])
            g = g[0:160, 0:128] + (g[0:160, 128:256] + (g[160:320, 0:128] + g[160:320, 128:256]))
            for lb in range(5):
                moved = V[lb, d] + g[lb * 32 : (lb + 1) * 32]
                new = moved - jnp.clip(moved, -SHRINK, SHRINK)
                new = jnp.where(k == steps - 1, moved, new)
                V[lb, d] = new if lb < 4 else jnp.where(keep, new, 0.0)
            return carry

        lax.fori_loop(0, 4, plane, 0, unroll=True)

    def rows16(g):
        return pl.ds(pl.multiple_of(g * 16, 16), 16)

    slot = p * 4 + z
    half1 = pl.ds(pl.multiple_of((1 - p) * 32, 32), 32)
    half2 = pl.ds(pl.multiple_of(p * 32, 32), 32)
    own = rows16(2 - p)

    def guarded(copy, ok):
        def run(verb):
            if ok is None:
                getattr(copy, verb)()
            else:
                @pl.when(ok)
                def _():
                    getattr(copy, verb)()

        return run

    def rs_copies(b):
        yield guarded(send(S.at[b, half2], rb2.at[slot], rs_send.at[b], rs2_recv.at[slot], owner2(b, kap)), None)
        for hx in (1, 0):
            h = (p + hx) % 2
            src = S.at[b, rows16((1 - p) * 2 + h)]
            copy = send(src, rb1.at[slot], rs_send.at[4 + hx * 4 + b], rs1_recv.at[slot], (2 * b + kap, 2 * c + h))
            yield guarded(copy, None if hx else z != b)

    def ag_arrived(b):
        came(R.at[b, half2], ag2_recv.at[b])
        for hx in range(2):
            h = (p + hx) % 2
            dst = R.at[b, rows16((1 - p) * 2 + h)]
            guarded(send(dst, dst, rs_send.at[0], ag1_recv.at[h, b], partner), None if hx else z != b)("wait_recv")

    lane8 = lane_of((8, LANES))

    def packed(total):
        x = jnp.where(kap == 0, pltpu.roll(total, 32, 1), total)
        y = x[0:8]
        for i in range(1, total.shape[0] // 8):
            y = jnp.where(lane8 < 32 * i, y, pltpu.roll(x[8 * i : 8 * i + 8], 32 * i, 1))
        return y

    def unpacked(y, rows):
        x = jnp.concatenate([pltpu.roll(y, (128 - 32 * i) % 128, 1) if i else y for i in range(rows // 8)], axis=0)
        lane = lane_of(x.shape)
        return jnp.where(
            kap == 0, jnp.where(lane < 32, x, 0.0), jnp.where(lane >= 96, pltpu.roll(x, 96, 1), 0.0)
        )

    def edge_rows(k):
        for h in range(2):
            came(px1.at[k, h], agx1_recv.at[k, h])
        came(px2.at[k], agx2_recv.at[k])
        one = jnp.concatenate([unpacked(px1[k, 0], 16), unpacked(px1[k, 1], 16)], axis=0)
        two = unpacked(px2[k], 32)
        return jnp.concatenate([jnp.where(p == 0, two, one), jnp.where(p == 0, one, two)], axis=0)

    def ag1_copies():
        for n, (h, b) in enumerate(around()):
            g = (1 - h) * 2 + p
            yield send(res1, R.at[z, rows16(g)], ag1_send.at[n], ag1_recv.at[p, z], (2 * b + kap, 2 * c + h))

    def agx1_copies(k):
        for h in range(2):
            for b in range(4):
                n = h * 4 + b
                yield send(ex1, px1.at[k, p], agx1_send.at[n], agx1_recv.at[k, p], (2 * b + other, 2 * c + h))

    def ag2_copies():
        for n, (tile, h, b) in enumerate(members2()):
            dst = R.at[block2, pl.ds(pl.multiple_of(h * 32, 32), 32)]
            yield send(res2, dst, ag2_send.at[n], ag2_recv.at[block2], (2 * b + kap, tile))

    def agx2_copies(k):
        for n, (tile, h, b) in enumerate(members2()):
            yield send(ex2, px2.at[k], agx2_send.at[n], agx2_recv.at[k], (2 * b + other, tile))

    def came(dst, sem):
        send(dst, dst, rs_send.at[0], sem, partner).wait_recv()

    def masked_edge(core):
        for j in range(4):
            V[4, core * 4 + j] = jnp.where(keep, V[4, core * 4 + j], 0.0)

    place_taps(kap)
    prep_forward(0, kap)
    for cp in loads:
        cp.wait()
    masked_edge(kap)
    pl.semaphore_wait(barrier, n_greets)
    give_raw.start()
    for cp in gives:
        cp.start()
    forward_planes(kap)
    take_raw.wait_recv()
    place_taps(other)
    prep_forward(0, other)
    for lb in range(5):
        came(V.at[lb, theirs], pair_recv.at[lb])
    masked_edge(other)
    forward_planes(other)
    forward_rows(0)
    give_raw.wait_send()
    for cp in gives:
        cp.wait_send()

    def finals():
        for lb in range(4):
            here = cols(kap * 4 + lb)
            yield send(V.at[lb, theirs], out.at[:, :, here], fin_send.at[lb], fin_recv.at[lb], partner)

    def finals_resid():
        for lb in range(4):
            here = cols(kap * 4 + lb)
            yield send(R.at[lb, 16:48], resid.at[:, here], fin_send.at[4 + lb], fin_recv.at[4 + lb], partner)
            yield pltpu.make_async_copy(R.at[lb, 16:48], resid.at[:, here], fin_loc.at[4 + lb])

    def finals_here():
        for lb in range(4):
            yield pltpu.make_async_copy(V.at[lb, mine], out.at[:, :, cols(kap * 4 + lb)], fin_loc.at[lb])

    def step(k, carry):
        prep_backward(k)

        @pl.when(inner)
        def _():
            total = jnp.zeros((32, LANES), F32)
            for q in range(8):
                came(rb2.at[q], rs2_recv.at[q])
                total = total + rb2[q]
            res2[...] = total
            for cp in ag2_copies():
                cp.start()

        @pl.when(edge2)
        def _():
            ex2[...] = packed(res2[...])
            for cp in agx2_copies(k):
                cp.start()

        total = S[z, own]
        for h, b in around():
            came(rb1.at[h * 4 + b], rs1_recv.at[h * 4 + b])
            total = total + rb1[h * 4 + b]
        res1[...] = total
        for cp in ag1_copies():
            cp.start()

        @pl.when(edge1)
        def _():
            ex1[...] = packed(total)
            for cp in agx1_copies(k):
                cp.start()

        R[z, own] = total
        nxt = jnp.minimum(k + 1, steps - 1)
        prep_forward(nxt, kap)
        prep_forward(nxt, other)
        for b in range(4):
            for cp in rs_copies(b):
                cp("wait_send")
        last = k == steps - 1

        backward_rows(k)

        @pl.when(last)
        def _():
            for cp in finals_resid():
                cp.start()

        backward_planes(k, other)

        @pl.when(last)
        def _():
            for cp in finals():
                cp.start()

        backward_planes(k, kap)
        for cp in ag1_copies():
            cp.wait_send()

        @pl.when(edge1)
        def _():
            for cp in agx1_copies(k):
                cp.wait_send()

        @pl.when(inner)
        def _():
            for cp in ag2_copies():
                cp.wait_send()

        @pl.when(edge2)
        def _():
            for cp in agx2_copies(k):
                cp.wait_send()

        @pl.when(jnp.logical_not(last))
        def _():
            forward_planes(kap)
            forward_planes(other)
            forward_rows(k + 1)

        return carry

    lax.fori_loop(0, steps, step, 0)
    for cp in finals_here():
        cp.start()
    for cp in (*finals_here(), *finals_resid(), *finals()):
        cp.wait()


def solution(mesh):
    nt = mesh.shape["tile"]

    def per_device(volume, measured, row_bank, col_bank, kernel_index, view_order):
        steps, rows, width = measured.shape
        vm, dma = pltpu.VMEM, pltpu.SemaphoreType.DMA
        anywhere = pl.BlockSpec(memory_space=pl.ANY)
        moved, resid = pl.pallas_call(
            functools.partial(kernel, nt, steps),
            name="ista",
            out_shape=(vm(volume.shape, F32), vm((rows, width), F32)),
            in_specs=[
                pl.BlockSpec(memory_space=pltpu.HBM),
                pl.BlockSpec(memory_space=pltpu.HBM),
                pl.BlockSpec(memory_space=vm),
                pl.BlockSpec(memory_space=vm),
                pl.BlockSpec(memory_space=pltpu.SMEM),
                pl.BlockSpec(memory_space=pltpu.SMEM),
            ],
            out_specs=(anywhere, anywhere),
            scratch_shapes=[
                vm((5, 8, rows, LANES), F32),
                vm((steps, rows, LANES), F32),
                vm((2, 4, 16, LANES), F32),
                vm((2, 4, 16, 640), F32),
                vm((8, 256, 256), BF16),
                vm((8, 256, 256), BF16),
                vm((8, 512, 256), BF16),
                vm((8, 64, LANES), F32),
                vm((128, 512), BF16),
                vm((8, 64, 256), BF16),
                vm((8, 64, 512), BF16),
                vm((8, 64, 512), BF16),
                vm((4, 64, LANES), F32),
                vm((2, 8, 64, 640), BF16),
                vm((8, 16, LANES), F32),
                vm((8, 32, LANES), F32),
                vm((16, LANES), F32),
                vm((32, LANES), F32),
                vm((8, LANES), F32),
                vm((8, LANES), F32),
                vm((4, 64, LANES), F32),
                vm((steps, 2, 8, LANES), F32),
                vm((steps, 8, LANES), F32),
                dma((12,)),
                dma((8,)),
                dma((8,)),
                dma((7,)),
                dma((8,)),
                dma((8,)),
                dma((8,)),
                dma((2, 4)),
                dma((4,)),
                dma((steps, 2)),
                dma((steps,)),
                dma((6,)),
                dma((5,)),
                dma((5,)),
                dma((2,)),
                dma((8,)),
                dma((8,)),
                dma((8,)),
            ],
            compiler_params=pltpu.CompilerParams(
                collective_id=0, has_side_effects=True, vmem_limit_bytes=61000 << 10
            ),
        )(volume, measured, row_bank.T, col_bank.T, kernel_index.T, view_order)
        return moved - jnp.clip(moved, -SHRINK, SHRINK), resid

    return jax.shard_map(
        per_device,
        mesh=mesh,
        in_specs=(P("depth", "tile", None), P(None, "tile", None), P(), P(), P(None, "depth"), P()),
        out_specs=(P("depth", "tile", None), P("tile", None)),
        check_vma=False,
    )
```

```python
import functools

import jax
import jax.numpy as jnp
from jax import lax
from jax.experimental import pallas as pl
from jax.experimental.pallas import tpu as pltpu
from jax.sharding import PartitionSpec as P

MESH = pl.DeviceIdType.MESH
DESCENT = 0.5
SHRINK = 0.1
LANES = 128
F32, BF16 = jnp.float32, jnp.bfloat16


def split(x):
    hi = x.astype(BF16)
    return hi, (x - hi.astype(F32)).astype(BF16)


def dot(a, b):
    return jnp.dot(a, b, preferred_element_type=F32)


def lane_of(shape):
    return lax.broadcasted_iota(jnp.int32, shape, len(shape) - 1)


def sheared(row, rows):
    wide = jnp.broadcast_to(row, (rows, row.shape[1]))
    return pltpu.roll(wide, 0, 1, stride=1, stride_axis=0)


def kernel(
    nt, steps,
    vol, meas, rowb, colb, kidx, vord,
    out, resid,
    V, mz, raw, H, TFh, TFl, TB, AF, A2, AP, Wh, Wl, S, XF, rb1, rb2, res1, res2, ex1, ex2, R, px1, px2,
    rs_send, rs1_recv, rs2_recv, ag1_send, ag2_send, agx1_send, agx2_send,
    ag1_recv, ag2_recv, agx1_recv, agx2_recv, loc_sem, pair_send, pair_recv, raw_sem, fin_loc, fin_send, fin_recv,
):
    dd, t = lax.axis_index("depth"), lax.axis_index("tile")
    kap, z = dd % 2, dd // 2
    p, c = t % 2, t // 2
    other = 1 - kap
    partner = (z * 2 + other, t)
    reach = (rowb.shape[0] - 1) // 2
    low2 = 2 * (c + p - 1)
    own2 = 2 * (c - p)
    inner = jnp.logical_or(z == 1, z == 2)
    pair2 = z - 1
    edge1 = z == 3 - 3 * kap
    edge2 = z == 2 - kap
    whole_src = jnp.logical_and(t != 0, t != nt - 1)
    whole_own = jnp.logical_and(t != 1, t != nt - 2)

    def wrapped(tile):
        return (tile + 2 * nt) % nt

    def owner2(h, pair, core):
        return ((1 + pair) * 2 + core, wrapped(low2 + 3 * h))

    FAR, NEAR = (4, 3, 5), (2, 6, 1, 7)

    def around(offsets=FAR + NEAR):
        for offset in offsets:
            place = (4 * p + z + offset) % 8
            yield place // 4, place % 4

    def members2(offsets=FAR + NEAR + (0,)):
        for offset in offsets:
            place = (4 * p + z + offset) % 8
            yield wrapped(own2 + 2 - place // 4), place // 4, place % 4

    def cols(block):
        return pl.ds(pl.multiple_of(block * LANES, LANES), LANES)

    def send(src, dst, s, r, dev):
        return pltpu.make_async_remote_copy(
            src_ref=src, dst_ref=dst, send_sem=s, recv_sem=r, device_id=dev, device_id_type=MESH
        )

    mine = pl.ds(kap * 4, 4)
    theirs = pl.ds(other * 4, 4)

    def block_of(core, lb):
        return core * 4 + lb if lb < 4 else 4 - core

    loads = [
        pltpu.make_async_copy(vol.at[:, :, cols(block_of(kap, lb))], V.at[lb, mine], loc_sem.at[lb])
        for lb in range(5)
    ]
    loads.append(pltpu.make_async_copy(meas.at[:, :, cols(kap * 4 + z)], mz, loc_sem.at[5]))
    for cp in loads:
        cp.start()
    gives = [
        send(vol.at[:, :, cols(block_of(other, lb))], V.at[lb, mine], pair_send.at[lb], pair_recv.at[lb], partner)
        for lb in range(5)
    ]
    R[...] = jnp.zeros_like(R)
    px2[...] = jnp.zeros_like(px2)
    barrier = pltpu.get_barrier_semaphore()

    def greet(dev):
        pl.semaphore_signal(barrier, inc=1, device_id=dev, device_id_type=MESH)

    greet(partner)
    for h, b in around():
        greet((2 * b + kap, 2 * c + h))
    for h in range(2):
        for pair in range(2):
            greet(owner2(h, pair, kap))
        greet((2 * (3 * kap) + other, 2 * c + h))
        greet(owner2(h, kap, other))

    @pl.when(edge1)
    def _():
        for h in range(2):
            for b in range(4):
                greet((2 * b + other, 2 * c + h))

    @pl.when(inner)
    def _():
        for tile, h, b in members2():
            greet((2 * b + kap, tile))

    @pl.when(edge2)
    def _():
        for tile, h, b in members2():
            greet((2 * b + other, tile))

    n_greets = 1 + 7 + 4 + 4 + 8 * (edge1.astype(jnp.int32) + inner.astype(jnp.int32) + edge2.astype(jnp.int32))

    taps = rowb.shape[0]
    j = lax.broadcasted_iota(jnp.int32, (16, rowb.shape[2]), 0)
    pick = jnp.zeros(j.shape, jnp.int32)
    for k in range(steps):
        view = vord[k]
        for d in range(4):
            pick = jnp.where(j == k * 4 + d, kidx[d, view], pick)
    onehot = (pick == lane_of(j.shape)).astype(F32)
    raw[kap] = jnp.zeros(raw.shape[1:], F32)
    for i, bank in enumerate((rowb, colb)):
        for r in range(2):
            raw[kap, 2 * i + r, :, 0:taps] = lax.dot_general(
                onehot, bank[:, r, :], (((1,), (1,)), ((), ())),
                precision=lax.Precision.HIGHEST, preferred_element_type=F32,
            )
    give_raw = send(raw.at[kap], raw.at[kap], raw_sem.at[0], raw_sem.at[1], partner)
    take_raw = send(raw.at[other], raw.at[other], raw_sem.at[0], raw_sem.at[1], partner)
    q = lax.broadcasted_iota(jnp.int32, (LANES, 640), 0)
    l = lax.broadcasted_iota(jnp.int32, (LANES, 640), 1)
    fwd = jnp.logical_and(l < 256, l == jnp.where(q <= reach, reach - q, 256 + reach - q))
    bwd = jnp.logical_and(
        jnp.logical_and(l >= 256, l < 512), l - 256 == jnp.where(q >= reach, q - reach, 256 + q - reach)
    )
    row = l - 512 == 2 * reach - q
    place = jnp.where(fwd | row, 1.0, jnp.where(bwd, -DESCENT, 0.0)).astype(F32)

    def place_taps(core):
        H[core] = jnp.dot(
            raw[core].reshape(-1, LANES), place, precision=lax.Precision.HIGHEST, preferred_element_type=F32
        ).reshape(H.shape[1:])

    lane32 = lane_of((32, LANES))
    low = lane32 < 64
    keep = low == (kap == 0)

    def taps_of(src, j, base, start, stop):
        rows = H[src, j, :, start:stop]
        mine = lax.broadcasted_iota(jnp.int32, rows.shape, 0) == base
        return jnp.sum(jnp.where(mine, rows, 0.0), axis=0, keepdims=True)

    def row_mats(k, d):
        base = k * 4 + d % 4
        for r in range(2):
            m = sheared(taps_of(d // 4, r, base, 512, 640), 32)
            m = jnp.where(jnp.logical_and(t == 0, lane32 < reach), 0.0, m)
            m = jnp.where(jnp.logical_and(t == nt - 1, lane32 >= 3 * reach), 0.0, m)
            yield r, m

    def prep_forward(k, core):
        def plane(j, carry):
            d = core * 4 + j
            base = k * 4 + d % 4
            for r in range(2):
                hi, lo = split(sheared(taps_of(d // 4, 2 + r, base, 0, 256), LANES))
                at = slice(r * LANES, (r + 1) * LANES)
                TFh[d, 0:128, at] = hi[:, 0:128]
                TFh[d, 128:256, at] = hi[:, 128:256]
                TFl[d, 0:128, at] = lo[:, 0:128]
                TFl[d, 128:256, at] = lo[:, 128:256]
            for r, m in row_mats(k, d):
                AF[d, r * 32 : (r + 1) * 32, :] = m
            return carry

        lax.fori_loop(0, 4, plane, 0, unroll=True)
        for j in range(2):
            m = AF[pl.ds(core * 4 + 2 * j, 2)].reshape(LANES, LANES).T[0:64]
            hi, lo = split(m)
            A2[0:64, cols(core * 2 + j)] = hi
            A2[64:128, cols(core * 2 + j)] = lo

    def prep_backward(k, core):
        def plane(j, carry):
            d = core * 4 + j
            base = k * 4 + d % 4
            for r in range(2):
                hi, lo = split(sheared(taps_of(d // 4, 2 + r, base, 256, 512), LANES))
                for e in range(2):
                    at = slice(e * 256 + r * LANES, e * 256 + (r + 1) * LANES)
                    TB[d, at, 0:128] = hi[:, e * 128 : (e + 1) * 128]
                    TB[d, at, 128:256] = lo[:, e * 128 : (e + 1) * 128]
            for r, m in row_mats(k, d):
                hi, lo = split(m)
                at = slice(r * 32, (r + 1) * 32)
                both = jnp.where(low, hi.astype(F32), pltpu.roll(lo.astype(F32), 64, 1))
                AP[d, at, 0:128] = both.astype(BF16)
                AP[d, at, 128:256] = hi
            return carry

        lax.fori_loop(0, 4, plane, 0, unroll=True)

    def forward_planes(core):
        def plane(j, carry):
            d = core * 4 + j
            v = [split(V[lb, d]) for lb in range(5)]
            hi, lo = (
                jnp.concatenate(
                    [
                        jnp.concatenate([v[lb][i], jnp.where(low, v[lb + 1][i], v[(lb + 4) % 5][i])], axis=1)
                        for lb in range(4)
                    ],
                    axis=0,
                )
                for i in range(2)
            )
            w = dot(jnp.concatenate([hi, lo], axis=0), TFh[d])
            w = w[0:128] + w[128:256] + dot(hi, TFl[d])
            hi, lo = split(w)
            for lb in range(4):
                for r in range(2):
                    src = (slice(lb * 32, (lb + 1) * 32), slice(r * 128, (r + 1) * 128))
                    dst = (d, slice(r * 32, (r + 1) * 32), slice(lb * 128, (lb + 1) * 128))
                    Wh[dst] = hi[src]
                    Wl[dst] = lo[src]
            return carry

        lax.fori_loop(0, 4, plane, 0, unroll=True)

    def forward_rows(k):
        for pair in range(2):
            at = slice(pair * 256, (pair + 1) * 256)
            s = dot(A2[...], Wh[:, :, at].reshape(512, 256))
            s = s[0:64] + s[64:128] + dot(A2[0:64], Wl[:, :, at].reshape(512, 256))
            for i in range(2):
                b = 2 * pair + i
                block = s[:, i * 128 : (i + 1) * 128]
                S[b, 0:16] = block[0:16]
                S[b, 16:48] = block[16:48] - jnp.where(z == b, mz[k], 0.0)
                S[b, 48:64] = block[48:64]
        for cp in rs_copies(0):
            cp("start")

    def backward_rows(k):
        ap = AP[...].reshape(512, 256)
        for pair in range(3):
            parts = []
            if pair < 2:
                ag_arrived(pair)
            for lb in range(2 * pair, min(2 * pair + 2, 5)):
                if lb < 4:
                    r = R[lb]
                else:
                    r = edge_rows(k)
                hi, lo = split(r)
                parts.append(jnp.concatenate([hi, hi, lo, lo], axis=0))
            x = dot(ap, jnp.concatenate(parts, axis=1)).reshape(8, 64, 128 * len(parts))
            hi, lo = split(x)
            at = slice(pair * 256, pair * 256 + 128 * len(parts))
            XF[0, :, :, at] = hi
            XF[1, :, :, at] = lo

    def backward_planes(k, core):
        def plane(j, carry):
            d = core * 4 + j
            rows = []
            for i in range(2):
                x = [
                    [XF[i, d, r * 32 : (r + 1) * 32, lb * 128 : (lb + 1) * 128] for r in range(2)] for lb in range(5)
                ]
                for lb in range(5):
                    near = [jnp.where(low, x[(lb + 1) % 5][r], x[(lb + 4) % 5][r]) for r in range(2)]
                    rows.append(jnp.concatenate(x[lb] + near, axis=1))
            g = dot(jnp.concatenate(rows, axis=0), TB[d])
            g = g[0:160, 0:128] + (g[0:160, 128:256] + (g[160:320, 0:128] + g[160:320, 128:256]))
            for lb in range(5):
                moved = V[lb, d] + g[lb * 32 : (lb + 1) * 32]
                new = moved - jnp.clip(moved, -SHRINK, SHRINK)
                new = jnp.where(k == steps - 1, moved, new)
                V[lb, d] = new if lb < 4 else jnp.where(keep, new, 0.0)
            return carry

        lax.fori_loop(0, 4, plane, 0, unroll=True)

    def rows16(g):
        return pl.ds(pl.multiple_of(g * 16, 16), 16)

    slot = p * 4 + z
    own = rows16(2 - p)

    def guarded(copy, ok):
        def run(verb):
            if ok is None:
                getattr(copy, verb)()
            else:
                @pl.when(ok)
                def _():
                    getattr(copy, verb)()

        return run

    def rs_copies(part):
        if part == 0:
            for i in range(4):
                h, pair = (p if i < 2 else 1 - p), i % 2
                src = S.at[2 * pair : 2 * pair + 2, rows16(2 * p + h)]
                copy = send(src, rb2.at[slot], rs_send.at[7 + i], rs2_recv.at[slot], owner2(h, pair, kap))
                yield guarded(copy, whole_src if i < 2 else None)
        for n, (h, b) in enumerate(around((FAR, NEAR)[part])):
            src = S.at[b, rows16((1 - p) * 2 + h)]
            copy = send(src, rb1.at[slot], rs_send.at[3 * part + n], rs1_recv.at[slot], (2 * b + kap, 2 * c + h))
            yield guarded(copy, None)

    def ag_arrived(pair):
        for hx in (1, 0):
            h = (p + hx) % 2
            for b in (2 * pair, 2 * pair + 1):
                dst = R.at[b, rows16((1 - p) * 2 + h)]
                guarded(send(dst, dst, rs_send.at[0], ag1_recv.at[h, b], partner), None if hx else z != b)("wait_recv")
            dst = R.at[2 * pair : 2 * pair + 2, rows16(2 * p + h)]
            guarded(send(dst, dst, rs_send.at[0], ag2_recv.at[h, pair], partner), None if hx else whole_src)("wait_recv")

    lane8 = lane_of((8, LANES))

    def packed(total):
        x = jnp.where(kap == 0, pltpu.roll(total, 32, 1), total)
        y = x[0:8]
        for i in range(1, total.shape[0] // 8):
            y = jnp.where(lane8 < 32 * i, y, pltpu.roll(x[8 * i : 8 * i + 8], 32 * i, 1))
        return y

    def unpacked(y, rows):
        x = jnp.concatenate([pltpu.roll(y, (128 - 32 * i) % 128, 1) if i else y for i in range(rows // 8)], axis=0)
        lane = lane_of(x.shape)
        return jnp.where(
            kap == 0, jnp.where(lane < 32, x, 0.0), jnp.where(lane >= 96, pltpu.roll(x, 96, 1), 0.0)
        )

    def edge_rows(k):
        for h in range(2):
            came(px1.at[k, h], agx1_recv.at[k, h])
        for hx in (1, 0):
            h = (p + hx) % 2
            dst = px2.at[k, h]
            guarded(send(dst, dst, rs_send.at[0], agx2_recv.at[k, h], partner), None if hx else whole_src)("wait_recv")
        one = jnp.concatenate([unpacked(px1[k, 0], 16), unpacked(px1[k, 1], 16)], axis=0)
        two = jnp.concatenate([unpacked(px2[k, 0], 16), unpacked(px2[k, 1], 16)], axis=0)
        return jnp.concatenate([jnp.where(p == 0, two, one), jnp.where(p == 0, one, two)], axis=0)

    def ag1_copies(part):
        for n, (h, b) in enumerate(around((FAR, NEAR)[part])):
            g = (1 - h) * 2 + p
            yield send(res1, R.at[z, rows16(g)], ag1_send.at[3 * part + n], ag1_recv.at[p, z], (2 * b + kap, 2 * c + h))

    def agx1_copies(k):
        for h in range(2):
            for b in range(4):
                n = h * 4 + b
                yield send(ex1, px1.at[k, p], agx1_send.at[n], agx1_recv.at[k, p], (2 * b + other, 2 * c + h))

    def ag2_copies(part):
        for n, (tile, h, b) in enumerate(members2((FAR + NEAR[:2], NEAR[2:] + (0,))[part])):
            dst = R.at[pl.ds(2 * pair2, 2), rows16(2 * h + p)]
            copy = send(res2, dst, ag2_send.at[5 * part + n], ag2_recv.at[p, pair2], (2 * b + kap, tile))
            yield guarded(copy, jnp.logical_or(whole_own, h != p))

    def agx2_copies(k):
        for n, (tile, h, b) in enumerate(members2()):
            copy = send(ex2, px2.at[k, p], agx2_send.at[n], agx2_recv.at[k, p], (2 * b + other, tile))
            yield guarded(copy, jnp.logical_or(whole_own, h != p))

    def came(dst, sem):
        send(dst, dst, rs_send.at[0], sem, partner).wait_recv()

    def masked_edge(core):
        for j in range(4):
            V[4, core * 4 + j] = jnp.where(keep, V[4, core * 4 + j], 0.0)

    place_taps(kap)
    prep_forward(0, kap)
    for cp in loads:
        cp.wait()
    masked_edge(kap)
    pl.semaphore_wait(barrier, n_greets)
    give_raw.start()
    for cp in gives:
        cp.start()
    forward_planes(kap)
    take_raw.wait_recv()
    place_taps(other)
    prep_forward(0, other)
    for lb in range(5):
        came(V.at[lb, theirs], pair_recv.at[lb])
    masked_edge(other)
    forward_planes(other)
    forward_rows(0)
    give_raw.wait_send()
    for cp in gives:
        cp.wait_send()

    def finals():
        for lb in range(4):
            here = cols(kap * 4 + lb)
            yield send(V.at[lb, theirs], out.at[:, :, here], fin_send.at[lb], fin_recv.at[lb], partner)

    def finals_resid():
        for lb in range(4):
            here = cols(kap * 4 + lb)
            yield send(R.at[lb, 16:48], resid.at[:, here], fin_send.at[4 + lb], fin_recv.at[4 + lb], partner)
            yield pltpu.make_async_copy(R.at[lb, 16:48], resid.at[:, here], fin_loc.at[4 + lb])

    def finals_here():
        for lb in range(4):
            yield pltpu.make_async_copy(V.at[lb, mine], out.at[:, :, cols(kap * 4 + lb)], fin_loc.at[lb])

    def step(k, carry):
        for cp in rs_copies(1):
            cp("start")
        prep_backward(k, kap)
        prep_backward(k, other)

        @pl.when(inner)
        def _():
            total = jnp.zeros((2, 16, LANES), F32)
            for _, h, b in members2():
                q, ok = h * 4 + b, jnp.logical_or(whole_own, h != p)
                guarded(send(res2, rb2.at[q], rs_send.at[0], rs2_recv.at[q], partner), ok)("wait_recv")
                total = total + jnp.where(ok, rb2[q], 0.0)
            res2[...] = total
            for cp in ag2_copies(0):
                cp("start")

        @pl.when(edge2)
        def _():
            ex2[...] = packed(jnp.where(kap == 0, res2[1], res2[0]))
            for cp in agx2_copies(k):
                cp("start")

        total = S[z, own]
        for h, b in around():
            came(rb1.at[h * 4 + b], rs1_recv.at[h * 4 + b])
            total = total + rb1[h * 4 + b]
        res1[...] = total
        for cp in ag1_copies(0):
            cp.start()

        @pl.when(edge1)
        def _():
            ex1[...] = packed(total)
            for cp in agx1_copies(k):
                cp.start()

        R[z, own] = total
        nxt = jnp.minimum(k + 1, steps - 1)
        for cp in ag1_copies(1):
            cp.start()

        @pl.when(inner)
        def _():
            for cp in ag2_copies(1):
                cp("start")

        prep_forward(nxt, kap)
        prep_forward(nxt, other)
        for cp in (*rs_copies(0), *rs_copies(1)):
            cp("wait_send")
        last = k == steps - 1

        backward_rows(k)

        @pl.when(last)
        def _():
            for cp in finals_resid():
                cp.start()

        backward_planes(k, other)

        @pl.when(last)
        def _():
            for cp in finals():
                cp.start()

        backward_planes(k, kap)
        for cp in (*ag1_copies(0), *ag1_copies(1)):
            cp.wait_send()

        @pl.when(edge1)
        def _():
            for cp in agx1_copies(k):
                cp.wait_send()

        @pl.when(inner)
        def _():
            for cp in (*ag2_copies(0), *ag2_copies(1)):
                cp("wait_send")

        @pl.when(edge2)
        def _():
            for cp in agx2_copies(k):
                cp("wait_send")

        @pl.when(jnp.logical_not(last))
        def _():
            forward_planes(kap)
            forward_planes(other)
            forward_rows(k + 1)

        return carry

    lax.fori_loop(0, steps, step, 0)
    for cp in finals_here():
        cp.start()
    for cp in (*finals_here(), *finals_resid(), *finals()):
        cp.wait()


def solution(mesh):
    nt = mesh.shape["tile"]

    def per_device(volume, measured, row_bank, col_bank, kernel_index, view_order):
        steps, rows, width = measured.shape
        vm, dma = pltpu.VMEM, pltpu.SemaphoreType.DMA
        anywhere = pl.BlockSpec(memory_space=pl.ANY)
        moved, resid = pl.pallas_call(
            functools.partial(kernel, nt, steps),
            name="ista",
            out_shape=(vm(volume.shape, F32), vm((rows, width), F32)),
            in_specs=[
                pl.BlockSpec(memory_space=pltpu.HBM),
                pl.BlockSpec(memory_space=pltpu.HBM),
                pl.BlockSpec(memory_space=vm),
                pl.BlockSpec(memory_space=vm),
                pl.BlockSpec(memory_space=pltpu.SMEM),
                pl.BlockSpec(memory_space=pltpu.SMEM),
            ],
            out_specs=(anywhere, anywhere),
            scratch_shapes=[
                vm((5, 8, rows, LANES), F32),
                vm((steps, rows, LANES), F32),
                vm((2, 4, 16, LANES), F32),
                vm((2, 4, 16, 640), F32),
                vm((8, 256, 256), BF16),
                vm((8, 256, 256), BF16),
                vm((8, 512, 256), BF16),
                vm((8, 64, LANES), F32),
                vm((128, 512), BF16),
                vm((8, 64, 256), BF16),
                vm((8, 64, 512), BF16),
                vm((8, 64, 512), BF16),
                vm((4, 64, LANES), F32),
                vm((2, 8, 64, 640), BF16),
                vm((8, 16, LANES), F32),
                vm((8, 2, 16, LANES), F32),
                vm((16, LANES), F32),
                vm((2, 16, LANES), F32),
                vm((8, LANES), F32),
                vm((8, LANES), F32),
                vm((4, 64, LANES), F32),
                vm((steps, 2, 8, LANES), F32),
                vm((steps, 2, 8, LANES), F32),
                dma((11,)),
                dma((8,)),
                dma((8,)),
                dma((7,)),
                dma((8,)),
                dma((8,)),
                dma((8,)),
                dma((2, 4)),
                dma((2, 2)),
                dma((steps, 2)),
                dma((steps, 2)),
                dma((6,)),
                dma((5,)),
                dma((5,)),
                dma((2,)),
                dma((8,)),
                dma((8,)),
                dma((8,)),
            ],
            compiler_params=pltpu.CompilerParams(
                collective_id=0, has_side_effects=True, vmem_limit_bytes=61000 << 10
            ),
        )(volume, measured, row_bank.T, col_bank.T, kernel_index.T, view_order)
        return moved - jnp.clip(moved, -SHRINK, SHRINK), resid

    return jax.shard_map(
        per_device,
        mesh=mesh,
        in_specs=(P("depth", "tile", None), P(None, "tile", None), P(), P(), P(None, "depth"), P()),
        out_specs=(P("depth", "tile", None), P("tile", None)),
        check_vma=False,
    )
```

```python
import functools

import jax
import jax.numpy as jnp
from jax import lax
from jax.experimental import pallas as pl
from jax.experimental.pallas import tpu as pltpu
from jax.sharding import PartitionSpec as P

MESH = pl.DeviceIdType.MESH
DESCENT = 0.5
SHRINK = 0.1
LANES = 128
F32, BF16 = jnp.float32, jnp.bfloat16


def split(x):
    hi = x.astype(BF16)
    return hi, (x - hi.astype(F32)).astype(BF16)


def dot(a, b):
    return jnp.dot(a, b, preferred_element_type=F32)


def lane_of(shape):
    return lax.broadcasted_iota(jnp.int32, shape, len(shape) - 1)


def sheared(row, rows):
    wide = jnp.broadcast_to(row, (rows, row.shape[1]))
    return pltpu.roll(wide, 0, 1, stride=1, stride_axis=0)


def kernel(
    nt, steps,
    vol, meas, rowb, colb, kidx, vord,
    out, resid,
    V, mz, raw, H, TFh, TFl, TB, AF, A2, AP, Wh, Wl, S, XF, rb1, rb2, res1, res2, ex1, ex2, R, px1, px2,
    rs_send, rs1_recv, rs2_recv, ag1_send, ag2_send, agx1_send, agx2_send,
    ag1_recv, ag2_recv, agx1_recv, agx2_recv, loc_sem, pair_send, pair_recv, raw_sem, fin_loc, fin_send, fin_recv,
):
    dd, t = lax.axis_index("depth"), lax.axis_index("tile")
    kap, z = dd % 2, dd // 2
    p, c = t % 2, t // 2
    other = 1 - kap
    partner = (z * 2 + other, t)
    reach = (rowb.shape[0] - 1) // 2
    low2 = 2 * (c + p - 1)
    own2 = 2 * (c - p)
    inner = jnp.logical_or(z == 1, z == 2)
    pair2 = z - 1
    edge1 = z == 3 - 3 * kap
    edge2 = z == 2 - kap
    whole_src = jnp.logical_and(t != 0, t != nt - 1)
    whole_own = jnp.logical_and(t != 1, t != nt - 2)

    def wrapped(tile):
        return (tile + 2 * nt) % nt

    def owner2(h, pair, core):
        return ((1 + pair) * 2 + core, wrapped(low2 + 3 * h))

    FAR, NEAR = (4, 3, 5), (2, 6, 1, 7)

    def around(offsets=FAR + NEAR):
        for offset in offsets:
            place = (4 * p + z + offset) % 8
            yield place // 4, place % 4

    def members2(offsets=FAR + NEAR + (0,)):
        for offset in offsets:
            place = (4 * p + z + offset) % 8
            yield wrapped(own2 + 2 - place // 4), place // 4, place % 4

    def cols(block):
        return pl.ds(pl.multiple_of(block * LANES, LANES), LANES)

    def send(src, dst, s, r, dev):
        return pltpu.make_async_remote_copy(
            src_ref=src, dst_ref=dst, send_sem=s, recv_sem=r, device_id=dev, device_id_type=MESH
        )

    R[...] = jnp.zeros_like(R)
    px2[...] = jnp.zeros_like(px2)
    barrier = pltpu.get_barrier_semaphore()

    def greet(dev):
        pl.semaphore_signal(barrier, inc=1, device_id=dev, device_id_type=MESH)

    for h, b in around():
        greet((2 * b + kap, 2 * c + h))
    for h in range(2):
        for pair in range(2):
            greet(owner2(h, pair, kap))
        greet((2 * (3 * kap) + other, 2 * c + h))
        greet(owner2(h, kap, other))

    @pl.when(edge1)
    def _():
        for h in range(2):
            for b in range(4):
                greet((2 * b + other, 2 * c + h))

    @pl.when(inner)
    def _():
        for tile, h, b in members2():
            greet((2 * b + kap, tile))

    @pl.when(edge2)
    def _():
        for tile, h, b in members2():
            greet((2 * b + other, tile))

    greet(partner)
    n_greets = 1 + 7 + 4 + 4 + 8 * (edge1.astype(jnp.int32) + inner.astype(jnp.int32) + edge2.astype(jnp.int32))

    mine = pl.ds(kap * 4, 4)
    theirs = pl.ds(other * 4, 4)

    def block_of(core, lb):
        return core * 4 + lb if lb < 4 else 4 - core

    loads = [
        pltpu.make_async_copy(vol.at[:, :, cols(block_of(kap, lb))], V.at[lb, mine], loc_sem.at[lb])
        for lb in range(5)
    ]
    loads.append(pltpu.make_async_copy(meas.at[:, :, cols(kap * 4 + z)], mz, loc_sem.at[5]))
    for cp in loads:
        cp.start()
    gives = [
        send(vol.at[:, :, cols(block_of(other, lb))], V.at[lb, mine], pair_send.at[lb], pair_recv.at[lb], partner)
        for lb in range(5)
    ]
    taps = rowb.shape[0]
    j = lax.broadcasted_iota(jnp.int32, (16, rowb.shape[2]), 0)
    pick = jnp.zeros(j.shape, jnp.int32)
    for k in range(steps):
        view = vord[k]
        for d in range(4):
            pick = jnp.where(j == k * 4 + d, kidx[d, view], pick)
    onehot = (pick == lane_of(j.shape)).astype(F32)
    raw[kap] = jnp.zeros(raw.shape[1:], F32)
    for i, bank in enumerate((rowb, colb)):
        for r in range(2):
            raw[kap, 2 * i + r, :, 0:taps] = lax.dot_general(
                onehot, bank[:, r, :], (((1,), (1,)), ((), ())),
                precision=lax.Precision.HIGHEST, preferred_element_type=F32,
            )
    give_raw = send(raw.at[kap], raw.at[kap], raw_sem.at[0], raw_sem.at[1], partner)
    take_raw = send(raw.at[other], raw.at[other], raw_sem.at[0], raw_sem.at[1], partner)
    q = lax.broadcasted_iota(jnp.int32, (LANES, 640), 0)
    l = lax.broadcasted_iota(jnp.int32, (LANES, 640), 1)
    fwd = jnp.logical_and(l < 256, l == jnp.where(q <= reach, reach - q, 256 + reach - q))
    bwd = jnp.logical_and(
        jnp.logical_and(l >= 256, l < 512), l - 256 == jnp.where(q >= reach, q - reach, 256 + q - reach)
    )
    row = l - 512 == 2 * reach - q
    place = jnp.where(fwd | row, 1.0, jnp.where(bwd, -DESCENT, 0.0)).astype(F32)

    def place_taps(core):
        H[core] = jnp.dot(
            raw[core].reshape(-1, LANES), place, precision=lax.Precision.HIGHEST, preferred_element_type=F32
        ).reshape(H.shape[1:])

    lane32 = lane_of((32, LANES))
    low = lane32 < 64
    keep = low == (kap == 0)

    def taps_of(src, j, base, start, stop):
        rows = H[src, j, :, start:stop]
        mine = lax.broadcasted_iota(jnp.int32, rows.shape, 0) == base
        return jnp.sum(jnp.where(mine, rows, 0.0), axis=0, keepdims=True)

    def row_mats(k, d):
        base = k * 4 + d % 4
        for r in range(2):
            m = sheared(taps_of(d // 4, r, base, 512, 640), 32)
            m = jnp.where(jnp.logical_and(t == 0, lane32 < reach), 0.0, m)
            m = jnp.where(jnp.logical_and(t == nt - 1, lane32 >= 3 * reach), 0.0, m)
            yield r, m

    def prep_forward(k, core):
        def plane(j, carry):
            d = core * 4 + j
            base = k * 4 + d % 4
            for r in range(2):
                hi, lo = split(sheared(taps_of(d // 4, 2 + r, base, 0, 256), LANES))
                at = slice(r * LANES, (r + 1) * LANES)
                TFh[d, 0:128, at] = hi[:, 0:128]
                TFh[d, 128:256, at] = hi[:, 128:256]
                TFl[d, 0:128, at] = lo[:, 0:128]
                TFl[d, 128:256, at] = lo[:, 128:256]
            for r, m in row_mats(k, d):
                AF[d, r * 32 : (r + 1) * 32, :] = m
            return carry

        lax.fori_loop(0, 4, plane, 0, unroll=True)
        for j in range(2):
            m = AF[pl.ds(core * 4 + 2 * j, 2)].reshape(LANES, LANES).T[0:64]
            hi, lo = split(m)
            A2[0:64, cols(core * 2 + j)] = hi
            A2[64:128, cols(core * 2 + j)] = lo

    def prep_backward(k, core):
        def plane(j, carry):
            d = core * 4 + j
            base = k * 4 + d % 4
            for r in range(2):
                hi, lo = split(sheared(taps_of(d // 4, 2 + r, base, 256, 512), LANES))
                for e in range(2):
                    at = slice(e * 256 + r * LANES, e * 256 + (r + 1) * LANES)
                    TB[d, at, 0:128] = hi[:, e * 128 : (e + 1) * 128]
                    TB[d, at, 128:256] = lo[:, e * 128 : (e + 1) * 128]
            for r, m in row_mats(k, d):
                hi, lo = split(m)
                at = slice(r * 32, (r + 1) * 32)
                both = jnp.where(low, hi.astype(F32), pltpu.roll(lo.astype(F32), 64, 1))
                AP[d, at, 0:128] = both.astype(BF16)
                AP[d, at, 128:256] = hi
            return carry

        lax.fori_loop(0, 4, plane, 0, unroll=True)

    def forward_planes(core):
        def plane(j, carry):
            d = core * 4 + j
            v = [split(V[lb, d]) for lb in range(5)]
            hi, lo = (
                jnp.concatenate(
                    [
                        jnp.concatenate([v[lb][i], jnp.where(low, v[lb + 1][i], v[(lb + 4) % 5][i])], axis=1)
                        for lb in range(4)
                    ],
                    axis=0,
                )
                for i in range(2)
            )
            w = dot(jnp.concatenate([hi, lo], axis=0), TFh[d])
            w = w[0:128] + w[128:256] + dot(hi, TFl[d])
            hi, lo = split(w)
            for lb in range(4):
                for r in range(2):
                    src = (slice(lb * 32, (lb + 1) * 32), slice(r * 128, (r + 1) * 128))
                    dst = (d, slice(r * 32, (r + 1) * 32), slice(lb * 128, (lb + 1) * 128))
                    Wh[dst] = hi[src]
                    Wl[dst] = lo[src]
            return carry

        lax.fori_loop(0, 4, plane, 0, unroll=True)

    def forward_rows(k):
        for pair in range(2):
            at = slice(pair * 256, (pair + 1) * 256)
            s = dot(A2[...], Wh[:, :, at].reshape(512, 256))
            s = s[0:64] + s[64:128] + dot(A2[0:64], Wl[:, :, at].reshape(512, 256))
            for i in range(2):
                b = 2 * pair + i
                block = s[:, i * 128 : (i + 1) * 128]
                S[b, 0:16] = block[0:16]
                S[b, 16:48] = block[16:48] - jnp.where(z == b, mz[k], 0.0)
                S[b, 48:64] = block[48:64]
        for cp in rs_copies(0):
            cp("start")

    def backward_rows(k):
        ap = AP[...].reshape(512, 256)
        for pair in range(3):
            parts = []
            if pair < 2:
                ag_arrived(pair)
            for lb in range(2 * pair, min(2 * pair + 2, 5)):
                if lb < 4:
                    r = R[lb]
                else:
                    r = edge_rows(k)
                hi, lo = split(r)
                parts.append(jnp.concatenate([hi, hi, lo, lo], axis=0))
            x = dot(ap, jnp.concatenate(parts, axis=1)).reshape(8, 64, 128 * len(parts))
            hi, lo = split(x)
            at = slice(pair * 256, pair * 256 + 128 * len(parts))
            XF[0, :, :, at] = hi
            XF[1, :, :, at] = lo

    def backward_planes(k, core):
        def plane(j, carry):
            d = core * 4 + j
            rows = []
            for i in range(2):
                x = [
                    [XF[i, d, r * 32 : (r + 1) * 32, lb * 128 : (lb + 1) * 128] for r in range(2)] for lb in range(5)
                ]
                for lb in range(5):
                    near = [jnp.where(low, x[(lb + 1) % 5][r], x[(lb + 4) % 5][r]) for r in range(2)]
                    rows.append(jnp.concatenate(x[lb] + near, axis=1))
            g = dot(jnp.concatenate(rows, axis=0), TB[d])
            g = g[0:160, 0:128] + (g[0:160, 128:256] + (g[160:320, 0:128] + g[160:320, 128:256]))
            for lb in range(5):
                moved = V[lb, d] + g[lb * 32 : (lb + 1) * 32]
                new = moved - jnp.clip(moved, -SHRINK, SHRINK)
                new = jnp.where(k == steps - 1, moved, new)
                V[lb, d] = new if lb < 4 else jnp.where(keep, new, 0.0)
            return carry

        lax.fori_loop(0, 4, plane, 0, unroll=True)

    def rows16(g):
        return pl.ds(pl.multiple_of(g * 16, 16), 16)

    slot = p * 4 + z
    own = rows16(2 - p)

    def guarded(copy, ok):
        def run(verb):
            if ok is None:
                getattr(copy, verb)()
            else:
                @pl.when(ok)
                def _():
                    getattr(copy, verb)()

        return run

    def rs_copies(part):
        if part == 0:
            for i in range(4):
                h, pair = (p if i < 2 else 1 - p), i % 2
                src = S.at[2 * pair : 2 * pair + 2, rows16(2 * p + h)]
                copy = send(src, rb2.at[slot], rs_send.at[7 + i], rs2_recv.at[slot], owner2(h, pair, kap))
                yield guarded(copy, whole_src if i < 2 else None)
        for n, (h, b) in enumerate(around((FAR, NEAR)[part])):
            src = S.at[b, rows16((1 - p) * 2 + h)]
            copy = send(src, rb1.at[slot], rs_send.at[3 * part + n], rs1_recv.at[slot], (2 * b + kap, 2 * c + h))
            yield guarded(copy, None)

    def ag_arrived(pair):
        for hx in (1, 0):
            h = (p + hx) % 2
            for b in (2 * pair, 2 * pair + 1):
                dst = R.at[b, rows16((1 - p) * 2 + h)]
                guarded(send(dst, dst, rs_send.at[0], ag1_recv.at[h, b], partner), None if hx else z != b)("wait_recv")
            dst = R.at[2 * pair : 2 * pair + 2, rows16(2 * p + h)]
            guarded(send(dst, dst, rs_send.at[0], ag2_recv.at[h, pair], partner), None if hx else whole_src)("wait_recv")

    lane8 = lane_of((8, LANES))

    def packed(total):
        x = jnp.where(kap == 0, pltpu.roll(total, 32, 1), total)
        y = x[0:8]
        for i in range(1, total.shape[0] // 8):
            y = jnp.where(lane8 < 32 * i, y, pltpu.roll(x[8 * i : 8 * i + 8], 32 * i, 1))
        return y

    def unpacked(y, rows):
        x = jnp.concatenate([pltpu.roll(y, (128 - 32 * i) % 128, 1) if i else y for i in range(rows // 8)], axis=0)
        lane = lane_of(x.shape)
        return jnp.where(
            kap == 0, jnp.where(lane < 32, x, 0.0), jnp.where(lane >= 96, pltpu.roll(x, 96, 1), 0.0)
        )

    def edge_rows(k):
        for h in range(2):
            came(px1.at[k, h], agx1_recv.at[k, h])
        for hx in (1, 0):
            h = (p + hx) % 2
            dst = px2.at[k, h]
            guarded(send(dst, dst, rs_send.at[0], agx2_recv.at[k, h], partner), None if hx else whole_src)("wait_recv")
        one = jnp.concatenate([unpacked(px1[k, 0], 16), unpacked(px1[k, 1], 16)], axis=0)
        two = jnp.concatenate([unpacked(px2[k, 0], 16), unpacked(px2[k, 1], 16)], axis=0)
        return jnp.concatenate([jnp.where(p == 0, two, one), jnp.where(p == 0, one, two)], axis=0)

    def ag1_copies(part):
        for n, (h, b) in enumerate(around((FAR, NEAR)[part])):
            g = (1 - h) * 2 + p
            yield send(res1, R.at[z, rows16(g)], ag1_send.at[3 * part + n], ag1_recv.at[p, z], (2 * b + kap, 2 * c + h))

    def agx1_copies(k):
        for h in range(2):
            for b in range(4):
                n = h * 4 + b
                yield send(ex1, px1.at[k, p], agx1_send.at[n], agx1_recv.at[k, p], (2 * b + other, 2 * c + h))

    def ag2_copies(part):
        for n, (tile, h, b) in enumerate(members2(((4, 2, 6, 3, 5), (1, 7, 0))[part])):
            dst = R.at[pl.ds(2 * pair2, 2), rows16(2 * h + p)]
            copy = send(res2, dst, ag2_send.at[5 * part + n], ag2_recv.at[p, pair2], (2 * b + kap, tile))
            yield guarded(copy, jnp.logical_or(whole_own, h != p))

    def agx2_copies(k):
        for n, (tile, h, b) in enumerate(members2()):
            copy = send(ex2, px2.at[k, p], agx2_send.at[n], agx2_recv.at[k, p], (2 * b + other, tile))
            yield guarded(copy, jnp.logical_or(whole_own, h != p))

    def came(dst, sem):
        send(dst, dst, rs_send.at[0], sem, partner).wait_recv()

    def masked_edge(core):
        for j in range(4):
            V[4, core * 4 + j] = jnp.where(keep, V[4, core * 4 + j], 0.0)

    place_taps(kap)
    prep_forward(0, kap)
    for cp in loads:
        cp.wait()
    masked_edge(kap)
    pl.semaphore_wait(barrier, n_greets)
    give_raw.start()
    for cp in gives:
        cp.start()
    forward_planes(kap)
    take_raw.wait_recv()
    place_taps(other)
    prep_forward(0, other)
    for lb in range(5):
        came(V.at[lb, theirs], pair_recv.at[lb])
    masked_edge(other)
    forward_planes(other)
    forward_rows(0)
    give_raw.wait_send()
    for cp in gives:
        cp.wait_send()

    def finals():
        for lb in range(4):
            here = cols(kap * 4 + lb)
            yield send(V.at[lb, theirs], out.at[:, :, here], fin_send.at[lb], fin_recv.at[lb], partner)

    def finals_resid():
        for lb in range(4):
            here = cols(kap * 4 + lb)
            yield send(R.at[lb, 16:48], resid.at[:, here], fin_send.at[4 + lb], fin_recv.at[4 + lb], partner)
            yield pltpu.make_async_copy(R.at[lb, 16:48], resid.at[:, here], fin_loc.at[4 + lb])

    def finals_here():
        for lb in range(4):
            yield pltpu.make_async_copy(V.at[lb, mine], out.at[:, :, cols(kap * 4 + lb)], fin_loc.at[lb])

    def ag_sent(k):
        for cp in (*ag1_copies(0), *ag1_copies(1)):
            cp.wait_send()

        @pl.when(edge1)
        def _():
            for cp in agx1_copies(k):
                cp.wait_send()

        @pl.when(inner)
        def _():
            for cp in (*ag2_copies(0), *ag2_copies(1)):
                cp("wait_send")

        @pl.when(edge2)
        def _():
            for cp in agx2_copies(k):
                cp("wait_send")

    def step(k, carry):
        for cp in rs_copies(1):
            cp("start")
        prep_backward(k, kap)
        prep_backward(k, other)

        @pl.when(k > 0)
        def _():
            ag_sent(k - 1)

        @pl.when(inner)
        def _():
            total = jnp.zeros((2, 16, LANES), F32)
            for _, h, b in members2():
                q, ok = h * 4 + b, jnp.logical_or(whole_own, h != p)
                guarded(send(res2, rb2.at[q], rs_send.at[0], rs2_recv.at[q], partner), ok)("wait_recv")
                total = total + jnp.where(ok, rb2[q], 0.0)
            res2[...] = total
            for cp in (*ag2_copies(0), *ag2_copies(1)):
                cp("start")

        total = S[z, own]
        for h, b in around():
            came(rb1.at[h * 4 + b], rs1_recv.at[h * 4 + b])
            total = total + rb1[h * 4 + b]
        res1[...] = total
        for cp in ag1_copies(0):
            cp.start()

        R[z, own] = total
        nxt = jnp.minimum(k + 1, steps - 1)
        for cp in ag1_copies(1):
            cp.start()

        @pl.when(edge2)
        def _():
            ex2[...] = packed(jnp.where(kap == 0, res2[1], res2[0]))
            for cp in agx2_copies(k):
                cp("start")

        @pl.when(edge1)
        def _():
            ex1[...] = packed(total)
            for cp in agx1_copies(k):
                cp.start()

        prep_forward(nxt, kap)
        prep_forward(nxt, other)
        for cp in (*rs_copies(0), *rs_copies(1)):
            cp("wait_send")
        last = k == steps - 1

        backward_rows(k)

        @pl.when(last)
        def _():
            for cp in finals_resid():
                cp.start()

        backward_planes(k, other)

        @pl.when(last)
        def _():
            for cp in finals():
                cp.start()

        backward_planes(k, kap)
        @pl.when(jnp.logical_not(last))
        def _():
            forward_planes(kap)
            forward_planes(other)
            forward_rows(k + 1)

        return carry

    lax.fori_loop(0, steps, step, 0)
    ag_sent(steps - 1)
    for cp in finals_here():
        cp.start()
    for cp in (*finals_here(), *finals_resid(), *finals()):
        cp.wait()


def solution(mesh):
    nt = mesh.shape["tile"]

    def per_device(volume, measured, row_bank, col_bank, kernel_index, view_order):
        steps, rows, width = measured.shape
        vm, dma = pltpu.VMEM, pltpu.SemaphoreType.DMA
        anywhere = pl.BlockSpec(memory_space=pl.ANY)
        moved, resid = pl.pallas_call(
            functools.partial(kernel, nt, steps),
            name="ista",
            out_shape=(vm(volume.shape, F32), vm((rows, width), F32)),
            in_specs=[
                pl.BlockSpec(memory_space=pltpu.HBM),
                pl.BlockSpec(memory_space=pltpu.HBM),
                pl.BlockSpec(memory_space=vm),
                pl.BlockSpec(memory_space=vm),
                pl.BlockSpec(memory_space=pltpu.SMEM),
                pl.BlockSpec(memory_space=pltpu.SMEM),
            ],
            out_specs=(anywhere, anywhere),
            scratch_shapes=[
                vm((5, 8, rows, LANES), F32),
                vm((steps, rows, LANES), F32),
                vm((2, 4, 16, LANES), F32),
                vm((2, 4, 16, 640), F32),
                vm((8, 256, 256), BF16),
                vm((8, 256, 256), BF16),
                vm((8, 512, 256), BF16),
                vm((8, 64, LANES), F32),
                vm((128, 512), BF16),
                vm((8, 64, 256), BF16),
                vm((8, 64, 512), BF16),
                vm((8, 64, 512), BF16),
                vm((4, 64, LANES), F32),
                vm((2, 8, 64, 640), BF16),
                vm((8, 16, LANES), F32),
                vm((8, 2, 16, LANES), F32),
                vm((16, LANES), F32),
                vm((2, 16, LANES), F32),
                vm((8, LANES), F32),
                vm((8, LANES), F32),
                vm((4, 64, LANES), F32),
                vm((steps, 2, 8, LANES), F32),
                vm((steps, 2, 8, LANES), F32),
                dma((11,)),
                dma((8,)),
                dma((8,)),
                dma((7,)),
                dma((8,)),
                dma((8,)),
                dma((8,)),
                dma((2, 4)),
                dma((2, 2)),
                dma((steps, 2)),
                dma((steps, 2)),
                dma((6,)),
                dma((5,)),
                dma((5,)),
                dma((2,)),
                dma((8,)),
                dma((8,)),
                dma((8,)),
            ],
            compiler_params=pltpu.CompilerParams(
                collective_id=0, has_side_effects=True, vmem_limit_bytes=61000 << 10
            ),
        )(volume, measured, row_bank.T, col_bank.T, kernel_index.T, view_order)
        return moved - jnp.clip(moved, -SHRINK, SHRINK), resid

    return jax.shard_map(
        per_device,
        mesh=mesh,
        in_specs=(P("depth", "tile", None), P(None, "tile", None), P(), P(), P(None, "depth"), P()),
        out_specs=(P("depth", "tile", None), P("tile", None)),
        check_vma=False,
    )
```
